32 devices in a mesh: fs: 8 (over z, x), pol: 4 (over y, core).
Axes of the slice: x: 2, y: 2, z: 4, core: 2. Of those that a mesh axis runs over, the one named last changes fastest.
Arguments:
- facets: bfloat16 [4, 64, 4096, 128], P('pol', 'fs'), may hold values from -6 to 6
- owners: int32 [64], replicated, may hold values from 0 to 7, as said below
- counts: int32 [64], replicated, may hold values from 1 to 8, as said below
- coords: float32 [2, 128, 8, 128], P(None, 'fs'), may hold values from 0 to 512
- station_ids: int32 [128, 8, 2, 128], P('fs'), may hold values from 0 to 511
- jones_table: float32 [8, 512], replicated, may hold values from -3 to 3
Outputs:
- predicted: float32 [4, 2, 128, 8, 128], P('pol', None, 'fs')
The draws below stay inside these ranges and needn't reach their ends.
Inputs may be any that keep to these rules, and one draw needn't show every extreme that they name: `owners`: each fs index owns at most 16 subgrids, and some index owns exactly 16. `counts`: some subgrid has exactly 8 blocks.
All inputs are finite; a program needn't handle non-finite values.
Results may differ from the reference program's by a relative error of at most 0.0055.
Values may be sent and summed in bfloat16 or wider, within the bound.
A program may use at most 128 MiB of HBM per device.

```python
import math
import jax
import jax.numpy as jnp
from jax import lax

R = 8
W = 64
S = 64
MAXB = 8
VB = 128
NST = 512
POLS = 4
F = 64
FH = 4096
SG = 512
CAP = 16
SLOTS = 128
N_FS = 8


def draw_owners(key, part):
    device_count = 2 * S // CAP
    base_load = CAP // 2
    key_order, key_shift, key_mix = jax.random.split(jax.random.fold_in(key, 11), 3)
    ordering = jax.random.permutation(key_order, device_count)
    shifts = jax.random.randint(key_shift, (device_count // 2,), 0, base_load + 1)
    shifts = shifts.at[0].set(base_load)
    device_loads = jnp.zeros((device_count,), jnp.int32)
    device_loads = device_loads.at[ordering[0::2]].set(base_load + shifts)
    device_loads = device_loads.at[ordering[1::2]].set(base_load - shifts)
    holders = jnp.repeat(jnp.arange(device_count, dtype=jnp.int32), device_loads, total_repeat_length=S)
    return holders[jax.random.permutation(key_mix, S)].astype(jnp.int32)


def draw_counts(key, part):
    key_values, key_place = jax.random.split(jax.random.fold_in(key, 23), 2)
    values = jax.random.randint(key_values, (S,), 1, MAXB + 1)
    position = jax.random.randint(key_place, (), 0, S)
    return values.at[position].set(MAXB).astype(jnp.int32)


def set_ends(entries, stream_key, least, largest):
    longest = entries.shape.index(max(entries.shape))
    spots = []
    for shift in (0, 1):
        where = [jax.random.randint(jax.random.fold_in(stream_key, axis), (), 0, length) for axis, length in enumerate(entries.shape)]
        where[longest] = (where[longest] + shift) % entries.shape[longest]
        spots.append(tuple(where))
    return entries.at[spots[0]].set(least).at[spots[1]].set(largest)


def block_scale(rng, shape, cuts, low, high):
    def one(axis_at, blocks):
        steps = jax.random.uniform(jax.random.fold_in(jax.random.fold_in(rng, 6), axis_at), (blocks,), jnp.float32, low / len(cuts), high / len(cuts))
        return jnp.repeat(jnp.exp(steps), shape[axis_at] // blocks).reshape((-1,) + (1,) * (len(shape) - axis_at - 1))

    gain = one(*cuts[0])
    for cut in cuts[1:]:
        gain = gain * one(*cut)
    return gain


def bell_draw(key, shape, deviation, bound, shards=(), held_as=jnp.bfloat16):
    entries = jax.random.normal(key, shape, jnp.float32) * deviation
    if len(shards) > 0:
        entries = block_scale(key, shape, shards, -0.22, 0.18) * entries
    return jnp.clip(entries, min=-bound, max=bound).astype(held_as)


def setup_inputs(seed: int = 0) -> dict:
    keys = jax.random.split(jax.random.key(seed), 7)
    facets = bell_draw(keys[0], (POLS, F, FH, 2 * W), 1.0, 6.0, ((0, 4), (1, 8)))
    owners = draw_owners(jax.random.fold_in(keys[6], 71), 0)
    counts = draw_counts(jax.random.fold_in(keys[6], 71), 0)
    coords = jnp.clip(512.0 * jax.random.uniform(keys[3], (2, SLOTS, MAXB, VB), jnp.float32) ** block_scale(keys[3], (2, SLOTS, MAXB, VB), ((1, 8),), -0.2, 0.2), 0.0, 512.0)
    station_ids = set_ends(jax.random.randint(keys[4], (SLOTS, MAXB, 2, VB), 0, NST), jax.random.fold_in(keys[4], 1), 0, NST - 1).astype(jnp.int32)
    jones_table = bell_draw(keys[5], (8, NST), 0.5, 3.0, (), jnp.float32)
    return dict(facets=facets, owners=owners, counts=counts, coords=coords, station_ids=station_ids, jones_table=jones_table)


def dft_tables(length):
    indices = jnp.arange(length, dtype=jnp.int32)
    phases = indices[:, None] * indices[None, :] % length
    angles = phases.astype(jnp.float32) * (2.0 * math.pi / length)
    return (jnp.cos(angles).astype(jnp.bfloat16), jnp.sin(angles).astype(jnp.bfloat16))

def turn_table(rows, cols, length):
    row_index = jnp.arange(rows, dtype=jnp.int32)
    col_index = jnp.arange(cols, dtype=jnp.int32)
    phases = row_index[:, None] * col_index[None, :] % length
    angles = phases.astype(jnp.float32) * (2.0 * math.pi / length)
    return (jnp.cos(angles), jnp.sin(angles))

def cell_phases(positions, cells):
    offsets = jnp.arange(cells, dtype=jnp.float32) - cells // 2
    angles = jnp.mod(positions[:, None] * offsets[None, :], float(cells)) * (2.0 * math.pi / cells)
    return (jnp.cos(angles), jnp.sin(angles))

def complex_product(left_real, left_imag, right_real, right_imag):
    return (left_real * right_real - left_imag * right_imag, left_real * right_imag + left_imag * right_real)

def reference(facets, owners, counts, coords, station_ids, jones_table):
    first_cos, first_sin = dft_tables(W)
    second_cos, second_sin = dft_tables(S)
    turn_cos, turn_sin = turn_table(W, S, FH)
    scale = 1.0 / math.sqrt(FH)
    flat_strips = facets.reshape(POLS * F, W, S, 2 * W)

    def transform(strip):
        cos_part = jnp.einsum('kn,nmc->kmc', first_cos, strip, preferred_element_type=jnp.float32)
        sin_part = jnp.einsum('kn,nmc->kmc', first_sin, strip, preferred_element_type=jnp.float32)
        section_real = cos_part[..., :W] + sin_part[..., W:]
        section_imag = cos_part[..., W:] - sin_part[..., :W]
        tc = turn_cos[:, :, None]
        ts = turn_sin[:, :, None]
        turned = jnp.concatenate([section_real * tc + section_imag * ts, section_imag * tc - section_real * ts], axis=2).astype(jnp.bfloat16)
        cos_two = jnp.einsum('qm,kmc->qkc', second_cos, turned, preferred_element_type=jnp.float32)
        sin_two = jnp.einsum('qm,kmc->qkc', second_sin, turned, preferred_element_type=jnp.float32)
        real_part = (cos_two[..., :W] + sin_two[..., W:]) * scale
        imag_part = (cos_two[..., W:] - sin_two[..., :W]) * scale
        return jnp.concatenate([real_part, imag_part], axis=2).reshape(FH, 2 * W).astype(jnp.bfloat16)
    windows = lax.map(transform, flat_strips).reshape(POLS, F, FH, 2 * W)
    owned = (owners[None, :] == jnp.arange(N_FS, dtype=jnp.int32)[:, None]).astype(jnp.int32)
    ranks = jnp.cumsum(owned, axis=1) - 1
    rank_of = lax.optimization_barrier(jnp.sum(owned * ranks, axis=0))
    slot_of = owners * CAP + rank_of

    def predict(index):
        tile = lax.dynamic_slice_in_dim(windows, index * W, W, axis=2)
        real_grid = tile[..., :W].reshape(POLS, R, R, W, W).transpose(0, 1, 3, 2, 4).reshape(POLS, SG, SG)
        imag_grid = tile[..., W:].reshape(POLS, R, R, W, W).transpose(0, 1, 3, 2, 4).reshape(POLS, SG, SG)
        grids = jnp.concatenate([real_grid, imag_grid], axis=2)
        positions = lax.dynamic_index_in_dim(coords, slot_of[index], axis=1, keepdims=False)
        row_cos, row_sin = cell_phases(positions[0].reshape(-1), SG)
        row_cos = row_cos.astype(jnp.bfloat16)
        row_sin = row_sin.astype(jnp.bfloat16)
        col_cos, col_sin = cell_phases(positions[1].reshape(-1), SG)
        results = []
        for pol_index in range(POLS):
            cos_part = jnp.dot(row_cos, grids[pol_index], preferred_element_type=jnp.float32)
            sin_part = jnp.dot(row_sin, grids[pol_index], preferred_element_type=jnp.float32)
            real_part = cos_part[:, :SG] + sin_part[:, SG:]
            imag_part = cos_part[:, SG:] - sin_part[:, :SG]
            vis_real = lax.optimization_barrier(jnp.sum(real_part * col_cos + imag_part * col_sin, axis=1)) / SG
            vis_imag = lax.optimization_barrier(jnp.sum(imag_part * col_cos - real_part * col_sin, axis=1)) / SG
            results.append(jnp.stack([vis_real, vis_imag]).reshape(2, MAXB, VB))
        return jnp.stack(results)
    per_subgrid = lax.map(predict, jnp.arange(S, dtype=jnp.int32))
    matches = owned[:, :, None] * (ranks[:, :, None] == jnp.arange(CAP, dtype=jnp.int32)[None, None, :]).astype(jnp.int32)
    slot_subgrid = lax.optimization_barrier(jnp.sum(matches * jnp.arange(S, dtype=jnp.int32)[None, :, None], axis=1)).reshape(-1)
    slot_valid = lax.optimization_barrier(jnp.sum(matches, axis=1)).reshape(-1)
    visible = jnp.take(per_subgrid, slot_subgrid, axis=0)
    block_limit = jnp.take(counts, slot_subgrid) * slot_valid
    keep = jnp.arange(MAXB, dtype=jnp.int32)[None, :] < block_limit[:, None]
    left = jnp.take(jones_table, station_ids[:, :, 0, :], axis=1)
    right = jnp.take(jones_table, station_ids[:, :, 1, :], axis=1)
    outputs = []
    for row_side in range(2):
        for col_side in range(2):
            total_real = jnp.zeros(visible.shape[:1] + visible.shape[3:], jnp.float32)
            total_imag = jnp.zeros(visible.shape[:1] + visible.shape[3:], jnp.float32)
            for inner_row in range(2):
                for inner_col in range(2):
                    left_entry = 2 * (2 * row_side + inner_row)
                    right_entry = 2 * (2 * col_side + inner_col)
                    comp_real = visible[:, 2 * inner_row + inner_col, 0]
                    comp_imag = visible[:, 2 * inner_row + inner_col, 1]
                    step_real, step_imag = complex_product(left[left_entry], left[left_entry + 1], comp_real, comp_imag)
                    step_real, step_imag = complex_product(step_real, step_imag, right[right_entry], -right[right_entry + 1])
                    total_real = total_real + step_real
                    total_imag = total_imag + step_imag
            outputs.append(jnp.stack([total_real, total_imag]))
    corrected = jnp.stack(outputs)
    return jnp.where(keep[None, None, :, :, None], corrected, 0.0)
```

```python
import functools
import math

import jax
import jax.numpy as jnp
import numpy as np
from jax import lax
from jax.experimental import pallas as pl
from jax.experimental.pallas import tpu as pltpu
from jax.sharding import PartitionSpec as P

R = 8
W = 64
S = 64
FH = 4096
SG = 512
LANES = 128
SPAN = 4
PITCH = 65
CHUNK = 1024
UNROLL = 8
PAIRS = 4


def fit(values, terms):
    series = np.polynomial.chebyshev.Chebyshev.interpolate(
        lambda square: values(np.sqrt(np.maximum(square, 1e-12))), terms - 1, domain=[0.0, 0.25]
    )
    return [float(c) for c in series.convert(kind=np.polynomial.Polynomial).coef]


SIN_COEFS = fit(lambda r: np.sin(np.pi * r) / r, 5)
COS_COEFS = fit(lambda r: np.cos(np.pi * r), 5)


def unit_circle(turns):
    return np.exp(-2j * np.pi * turns)


def as_real(table):
    return np.concatenate(
        [
            np.concatenate([table.real, -table.imag], axis=-1),
            np.concatenate([table.imag, table.real], axis=-1),
        ],
        axis=-2,
    )


def mix_table():
    table = np.zeros((4 * W, 4 * W))
    col = np.arange(W)
    mirror = W - 1 - col
    a_real, a_imag, b_real, b_imag = mirror, W + mirror, 2 * W + col, 3 * W + col
    table[b_real, col] = table[a_real, col] = 1.0
    table[b_imag, W + col] = 1.0
    table[a_imag, W + col] = -1.0
    table[b_imag, 2 * W + col] = table[a_imag, 2 * W + col] = 1.0
    table[b_real, 3 * W + col] = -1.0
    table[a_real, 3 * W + col] = 1.0
    return table


def first_tables():
    n1 = np.arange(S)[:, None, None]
    k1 = np.arange(W)[None, :, None]
    n2 = np.arange(W)[None, None, :]
    rows = unit_circle((k1 * n2 % W) / W + (n1 * k1 % FH) / FH)
    upper, lower = rows[:, W // 2 :], rows[:, W // 2 - 1 :: -1]
    return as_real(np.concatenate([upper + lower, -1j * (upper - lower)], axis=1))


def second_table():
    index = np.arange(S)
    table = unit_circle((index[:, None] * index[None, :] % S) / S)
    return as_real(table) / (math.sqrt(FH) * SG)


def horner(coefs, square):
    total = jnp.full_like(square, coefs[-1])
    for coef in coefs[-2::-1]:
        total = total * square + coef
    return total


def phase(turns):
    rest = turns - jnp.round(turns)
    square = rest * rest
    half_cos = horner(COS_COEFS, square)
    half_sin = horner(SIN_COEFS, square) * rest
    double = half_sin + half_sin
    return 1.0 - double * half_sin, double * half_cos


def twice(left, right):
    return (left[0] * right[0] - left[1] * right[1], left[1] * right[0] + left[0] * right[1])


def chain(start, step, count):
    terms = [start, twice(start, step)]
    double = step[0] + step[0]
    while len(terms) < count:
        (last_cos, last_sin), (cos, sin) = terms[-2:]
        terms.append((double * cos - last_cos, double * sin - last_sin))
    return terms


def transform_kernel(
    device_count, strips_ref, first_hbm, coords_ref, mix_ref, second_ref, out_ref, gathered_ref,
    strip_ref, first_ref, mixed_ref, turned_ref, everyone_ref, strip_sem, first_sem, own_sem,
    send_sem, recv_sem, pair_send_sem, pair_recv_sem
):
    me = lax.axis_index("fs")
    pol = lax.axis_index("pol")
    half = lax.rem(pol, 2)
    partner = {"pol": pol + 1 - 2 * half}
    facet_local = strip_ref.shape[0]
    slots = everyone_ref.shape[2] // 2
    span = min(SPAN, facet_local)
    pairs = span // 2

    order = []
    for group in range(facet_local // span):
        for pair in range(pairs):
            low = group * span + pairs - 1 - pair
            order.append((low, low + 2 * pair + 1))
    loads = [
        pltpu.make_async_copy(strips_ref.at[f], strip_ref.at[f], strip_sem.at[f])
        for f in range(facet_local)
    ]
    for low, high in order:
        loads[low].start()
        loads[high].start()
    tables = pltpu.make_async_copy(first_hbm, first_ref, first_sem)
    tables.start()
    own = pltpu.make_async_copy(coords_ref, everyone_ref.at[me], own_sem)
    own.start()

    barrier = pltpu.get_barrier_semaphore()
    for step in range(1, device_count):
        pl.semaphore_signal(
            barrier,
            inc=1,
            device_id={"fs": lax.rem(me + step, device_count)},
            device_id_type=pl.DeviceIdType.MESH,
        )
    pl.semaphore_signal(barrier, inc=1, device_id=partner, device_id_type=pl.DeviceIdType.MESH)
    pl.semaphore_wait(barrier, device_count)
    own.wait()
    sends = []
    for step in range(1, device_count):
        mine = everyone_ref.at[me, :, pl.ds(half * slots, slots)]
        copy = pltpu.make_async_remote_copy(
            src_ref=mine,
            dst_ref=mine,
            send_sem=send_sem.at[step - 1],
            recv_sem=recv_sem.at[step - 1],
            device_id={"fs": lax.rem(me + step, device_count)},
            device_id_type=pl.DeviceIdType.MESH,
        )
        copy.start()
        sends.append(copy)

    def lanes(pieces):
        return jnp.concatenate(pieces, axis=1).astype(jnp.bfloat16)

    for group in range(facet_local // span):
        for pair in range(pairs):
            low, high = order[group * pairs + pair]
            loads[low].wait()
            loads[high].wait()

            def mix(i, carry, low=low, high=high, pair=pair):
                rows = pl.ds(pl.multiple_of(i * CHUNK, CHUNK), CHUNK)
                both = jnp.dot(
                    jnp.concatenate([strip_ref[low, rows, :], strip_ref[high, rows, :]], axis=1),
                    mix_ref[...],
                    preferred_element_type=jnp.float32,
                )
                for t in range(CHUNK // W):
                    to = pl.ds((i * (CHUNK // W) + t) * PITCH, W)
                    for part in range(2):
                        mixed_ref[2 * pair + part, to, :] = both[
                            W * t : W * (t + 1), LANES * part : LANES * (part + 1)
                        ]
                return carry

            lax.fori_loop(0, FH // CHUNK, mix, 0)
        if group == 0:
            tables.wait()

        def put(to_ref, rows, product):
            for pair in range(pairs):
                for part in range(2):
                    to_ref[2 * pair + part, rows, :] = product[
                        W * part : W * (part + 1), LANES * pair : LANES * (pair + 1)
                    ]

        def take(from_ref, rows):
            return jnp.concatenate(
                [lanes([from_ref[2 * q + part, rows, :] for q in range(pairs)]) for part in range(2)],
                axis=0,
            )

        def first(i, carry):
            for u in range(UNROLL):
                rows = pl.ds(i * UNROLL + u, W, stride=PITCH)
                put(
                    turned_ref,
                    rows,
                    jnp.dot(
                        first_ref[i * UNROLL + u],
                        take(mixed_ref, rows),
                        preferred_element_type=jnp.float32,
                    ),
                )
            return carry

        lax.fori_loop(0, S // UNROLL, first, 0)

        def second(i, carry):
            for u in range(UNROLL):
                k = i * UNROLL + u
                put(
                    mixed_ref,
                    pl.ds(k, S, stride=PITCH),
                    jnp.dot(
                        second_ref[...],
                        take(turned_ref, pl.ds(k * PITCH, S)),
                        preferred_element_type=jnp.float32,
                    ),
                )
            return carry

        lax.fori_loop(0, W // UNROLL, second, 0)

        def third(i, carry, group=group):
            for u in range(2):
                s = i * 2 + u
                out_ref[s, pl.ds(group * 2 * W, 2 * W), :] = take(mixed_ref, pl.ds(s * PITCH, W))
            return carry

        lax.fori_loop(0, S // 2, third, 0)

    forwards = []
    for step in range(1, device_count):
        sends[step - 1].wait_recv()
        theirs = everyone_ref.at[
            lax.rem(me + device_count - step, device_count), :, pl.ds(half * slots, slots)
        ]
        copy = pltpu.make_async_remote_copy(
            src_ref=theirs,
            dst_ref=theirs,
            send_sem=pair_send_sem.at[step - 1],
            recv_sem=pair_recv_sem.at[step - 1],
            device_id=partner,
            device_id_type=pl.DeviceIdType.MESH,
        )
        copy.start()
        forwards.append(copy)
    for copy in forwards:
        copy.wait_recv()
    for copy in sends + forwards:
        copy.wait_send()
    gathered_ref[...] = everyone_ref[...]


def transform(strips, coords, device_count):
    vmem = pl.BlockSpec(memory_space=pltpu.VMEM)
    anywhere = pl.BlockSpec(memory_space=pl.ANY)
    facet_local = strips.shape[0]
    span = min(SPAN, facet_local)
    scratch = pltpu.VMEM((span, S * PITCH, LANES), jnp.float32)
    constant = lambda table: jnp.asarray(table, jnp.bfloat16)
    return pl.pallas_call(
        functools.partial(transform_kernel, device_count),
        out_shape=[
            jax.ShapeDtypeStruct((S, facet_local // span * 2 * W, span * W), jnp.bfloat16),
            jax.ShapeDtypeStruct((device_count,) + coords.shape, jnp.float32),
        ],
        in_specs=[anywhere, anywhere, anywhere, vmem, vmem],
        out_specs=[vmem, vmem],
        scratch_shapes=[
            pltpu.VMEM((facet_local, FH, LANES), jnp.bfloat16),
            pltpu.VMEM((S, 2 * W, 2 * W), jnp.bfloat16),
            scratch,
            scratch,
            pltpu.VMEM((device_count,) + coords.shape, jnp.float32),
            pltpu.SemaphoreType.DMA((facet_local,)),
            pltpu.SemaphoreType.DMA,
            pltpu.SemaphoreType.DMA,
            pltpu.SemaphoreType.DMA((device_count - 1,)),
            pltpu.SemaphoreType.DMA((device_count - 1,)),
            pltpu.SemaphoreType.DMA((device_count - 1,)),
            pltpu.SemaphoreType.DMA((device_count - 1,)),
        ],
        compiler_params=pltpu.CompilerParams(
            vmem_limit_bytes=42 * 2**20, collective_id=0, has_side_effects=True
        ),
        cost_estimate=pl.CostEstimate(
            flops=5 * 10**9, bytes_accessed=16 * 2**20, transcendentals=0
        ),
    )(strips, constant(first_tables()), coords, constant(mix_table()), constant(second_table()))


def predict_kernel(
    facet_local, index_ref, owners_ref, counts_ref, coords_ref, windows_ref, parts_ref, out_ref,
    table_ref, row_ref, place_ref, loads_ref
):
    device_count = out_ref.shape[0]
    lane = out_ref.shape[4]
    subgrids = owners_ref.shape[0]
    span = min(SPAN, facet_local)
    groups = facet_local // span
    steps = span // 2
    first = index_ref[0] * facet_local
    unit = 1.0 / SG
    row_middle = (lax.div(first, R) * W).astype(jnp.float32) + (0.5 * (W - 1) - SG // 2)
    col_middle = (lax.rem(first, R) * W).astype(jnp.float32) + (0.5 * (span * W - 1) - SG // 2)
    ramp = lax.broadcasted_iota(jnp.int32, (8, lane), 0).astype(jnp.float32)
    fine = (ramp + 0.5) * unit
    col_pick = jnp.where(ramp == 1.0, 0.0, col_middle + (ramp - 2.0) * (span * W))
    col_pick = jnp.where(ramp == 0.0, 8.0, col_pick) * unit
    row_pick = jnp.where(ramp == 0.0, 0.0, jnp.where(ramp == 1.0, 8.0, row_middle)) * unit
    out_ref[...] = jnp.zeros_like(out_ref)

    def clear(i, carry):
        loads_ref[i] = 0
        return carry

    lax.fori_loop(0, device_count, clear, 0)

    def rank(s, total):
        owner = owners_ref[s]
        load = loads_ref[owner]
        loads_ref[owner] = load + 1
        place_ref[s] = load
        return total + lax.div(counts_ref[s] + 1, 2)

    total = lax.fori_loop(0, subgrids, rank, 0)

    def following(s, b):
        items = []
        for _ in range(PAIRS):
            items.append((s, b))
            done = b + 2 >= counts_ref[s]
            end = jnp.logical_and(done, s == subgrids - 1)
            b = jnp.where(end, b, jnp.where(done, 0, b + 2))
            s = jnp.where(done, jnp.minimum(s + 1, subgrids - 1), s)
        return items, (s, b)

    def tables(u, turn, s, b):
        owner, load = owners_ref[s], place_ref[s]
        for h in range(2):
            x = coords_ref[owner, 0, load, pl.ds(b + h, 1), :]
            y = coords_ref[owner, 1, load, pl.ds(b + h, 1), :]
            picked = phase(x * row_pick + y * col_pick)
            col_step, row_step = [
                [jnp.broadcast_to(part[i : i + 1], (8, lane)) for part in picked] for i in range(2)
            ]
            cols = chain(phase(y * fine), col_step, steps * W // 8)
            entries = []
            for k in range(steps):
                some = cols[W // 8 * k : W // 8 * (k + 1)]
                entries += [cos for cos, _ in some] + [sin for _, sin in some]
            table_ref[u, :, h * lane : (h + 1) * lane] = jnp.concatenate(entries, axis=0).astype(
                jnp.bfloat16
            )
            rows = chain(phase(x * fine), row_step, W // 16)
            row_ref[turn, u, h] = jnp.concatenate(
                [cos for cos, _ in rows] + [sin for _, sin in rows] + list(picked), axis=0
            )

    def predict(u, turn, s, b):
        grid = jnp.dot(windows_ref[s], table_ref[u], preferred_element_type=jnp.float32)
        owner, load = owners_ref[s], place_ref[s]
        for h in range(2):
            real = imag = None
            for g in range(groups):
                sums = []
                for part in range(2):
                    total = None
                    for k in range(W // 8):
                        at = (2 * g + part) * W + 8 * k
                        term = grid[at : at + 8, h * lane : (h + 1) * lane] * row_ref[
                            turn, u, h, 8 * k : 8 * k + 8, :
                        ]
                        total = term if total is None else total + term
                    sums.append(total)
                cos = row_ref[turn, u, h, W + 2 + g : W + 3 + g, :]
                sin = row_ref[turn, u, h, W + 10 + g : W + 11 + g, :]
                more_real = sums[0] * cos + sums[1] * sin
                more_imag = sums[1] * cos - sums[0] * sin
                real = more_real if real is None else real + more_real
                imag = more_imag if imag is None else imag + more_imag
            out_ref[owner, load, 0, pl.ds(b + h, 1), :] = jnp.sum(real, axis=0, keepdims=True)
            out_ref[owner, load, 1, pl.ds(b + h, 1), :] = jnp.sum(imag, axis=0, keepdims=True)

    items, after = following(0, 0)
    for u, (s, b) in enumerate(items):
        tables(u, 0, s, b)

    def step(i, carry):
        items, after = carry
        for u, (s, b) in enumerate(items):
            predict(u, i & 1, s, b)
        items, after = following(*after)
        for u, (s, b) in enumerate(items):
            tables(u, (i + 1) & 1, s, b)
        return items, after

    lax.fori_loop(0, lax.div(total + PAIRS - 1, PAIRS), step, (items, after))
    parts_ref[...] = out_ref[...].astype(jnp.bfloat16)


def predict(windows, owners, counts, coords, device_index, facet_local):
    device_count, _, capacity, max_blocks, lane = coords.shape
    smem = pl.BlockSpec(memory_space=pltpu.SMEM)
    vmem = pl.BlockSpec(memory_space=pltpu.VMEM)
    slots = (device_count, capacity, 2, max_blocks, lane)
    return pl.pallas_call(
        functools.partial(predict_kernel, facet_local),
        out_shape=jax.ShapeDtypeStruct(slots, jnp.bfloat16),
        in_specs=[smem, smem, smem, vmem, vmem],
        out_specs=vmem,
        scratch_shapes=[
            pltpu.VMEM(slots, jnp.float32),
            pltpu.VMEM((PAIRS, windows.shape[2], 2 * lane), jnp.bfloat16),
            pltpu.VMEM((2, PAIRS, 2, W + 16, lane), jnp.float32),
            pltpu.SMEM((owners.shape[0],), jnp.int32),
            pltpu.SMEM((device_count,), jnp.int32),
        ],
        compiler_params=pltpu.CompilerParams(vmem_limit_bytes=16 * 2**20),
    )(device_index.reshape(1), owners, counts, coords, windows)


def add_up_kernel(
    device_count, pols, in_ref, out_ref, arrived_ref, total_ref, send_sem, recv_sem, pol_send_sem,
    pol_recv_sem
):
    me = lax.axis_index("fs")
    pol = lax.axis_index("pol")
    peers = [{"fs": lax.rem(me + step, device_count)} for step in range(1, device_count)]
    pol_peers = [{"pol": lax.rem(pol + step, pols)} for step in range(1, pols)]
    barrier = pltpu.get_barrier_semaphore()
    for peer in peers + pol_peers:
        pl.semaphore_signal(
            barrier, inc=1, device_id=peer, device_id_type=pl.DeviceIdType.MESH
        )
    pl.semaphore_wait(barrier, device_count + pols - 2)
    copies = []
    for i, peer in enumerate(peers):
        copy = pltpu.make_async_remote_copy(
            src_ref=in_ref.at[peer["fs"]],
            dst_ref=arrived_ref.at[i],
            send_sem=send_sem.at[i],
            recv_sem=recv_sem.at[i],
            device_id=peer,
            device_id_type=pl.DeviceIdType.MESH,
        )
        copy.start()
        copies.append(copy)
    total_ref[pol] = in_ref[me].astype(jnp.float32)
    for i, copy in enumerate(copies):
        copy.wait_recv()
        total_ref[pol] += arrived_ref[i].astype(jnp.float32)
    pol_copies = []
    for i, peer in enumerate(pol_peers):
        copy = pltpu.make_async_remote_copy(
            src_ref=total_ref.at[pol],
            dst_ref=total_ref.at[pol],
            send_sem=pol_send_sem.at[i],
            recv_sem=pol_recv_sem.at[i],
            device_id=peer,
            device_id_type=pl.DeviceIdType.MESH,
        )
        copy.start()
        pol_copies.append(copy)
    for copy in pol_copies:
        copy.wait_recv()
    for copy in copies + pol_copies:
        copy.wait_send()
    out_ref[...] = total_ref[...]


def add_up(parts, pols):
    device_count = parts.shape[0]
    vmem = pl.BlockSpec(memory_space=pltpu.VMEM)
    return pl.pallas_call(
        functools.partial(add_up_kernel, device_count, pols),
        out_shape=jax.ShapeDtypeStruct((pols,) + parts.shape[1:], jnp.float32),
        in_specs=[vmem],
        out_specs=vmem,
        scratch_shapes=[
            pltpu.VMEM((device_count - 1,) + parts.shape[1:], jnp.bfloat16),
            pltpu.VMEM((pols,) + parts.shape[1:], jnp.float32),
            pltpu.SemaphoreType.DMA((device_count - 1,)),
            pltpu.SemaphoreType.DMA((device_count - 1,)),
            pltpu.SemaphoreType.DMA((pols - 1,)),
            pltpu.SemaphoreType.DMA((pols - 1,)),
        ],
        compiler_params=pltpu.CompilerParams(collective_id=1, has_side_effects=True),
    )(parts)


def correct_kernel(index_ref, owners_ref, counts_ref, left_ref, right_ref, table_ref, vis_ref, out_ref):
    capacity = out_ref.shape[1]
    max_blocks, lane = out_ref.shape[2:]
    chunks = table_ref.shape[1] // lane
    me = index_ref[0]
    out_ref[...] = jnp.zeros_like(out_ref)
    block = lax.broadcasted_iota(jnp.int32, (max_blocks, lane), 0)

    def look_up(first, ids):
        low = ids % lane
        high = ids // lane
        found = []
        for row in range(4):
            entry = None
            for chunk in range(chunks):
                source = jnp.broadcast_to(
                    table_ref[first + row : first + row + 1, chunk * lane : (chunk + 1) * lane],
                    (max_blocks, lane),
                )
                got = jnp.take_along_axis(source, low, axis=1, mode="promise_in_bounds")
                entry = got if entry is None else jnp.where(high == chunk, got, entry)
            found.append(entry)
        return [(found[0], found[1]), (found[2], found[3])]

    def product(a, b):
        return (a[0] * b[0] - a[1] * b[1], a[0] * b[1] + a[1] * b[0])

    def slot(s, load):
        is_mine = owners_ref[s] == me

        @pl.when(is_mine)
        def _():
            left = look_up(0, left_ref[load])
            right = look_up(4, right_ref[load])
            total_real = jnp.zeros((max_blocks, lane), jnp.float32)
            total_imag = jnp.zeros((max_blocks, lane), jnp.float32)
            for inner_row in range(2):
                for inner_col in range(2):
                    comp = 2 * inner_row + inner_col
                    step = product(
                        left[inner_row], (vis_ref[comp, load, 0], vis_ref[comp, load, 1])
                    )
                    step = product(step, (right[inner_col][0], -right[inner_col][1]))
                    total_real = total_real + step[0]
                    total_imag = total_imag + step[1]
            keep = block < counts_ref[s]
            out_ref[0, load] = jnp.where(keep, total_real, 0.0)
            out_ref[1, load] = jnp.where(keep, total_imag, 0.0)

        return load + is_mine.astype(jnp.int32)

    lax.fori_loop(0, owners_ref.shape[0], slot, 0)


def correct(visible, owners, counts, station_ids, tables, device_index):
    _, capacity, _, max_blocks, lane = visible.shape
    smem = pl.BlockSpec(memory_space=pltpu.SMEM)
    vmem = pl.BlockSpec(memory_space=pltpu.VMEM)
    return pl.pallas_call(
        correct_kernel,
        out_shape=jax.ShapeDtypeStruct((2, capacity, max_blocks, lane), jnp.float32),
        in_specs=[smem, smem, smem, vmem, vmem, vmem, vmem],
        out_specs=vmem,
    )(
        device_index.reshape(1),
        owners,
        counts,
        station_ids[:, :, 0, :],
        station_ids[:, :, 1, :],
        tables,
        visible,
    )


def on_device(facets, owners, counts, coords, station_ids, jones_table):
    device_index = lax.axis_index("fs").astype(jnp.int32)
    pol_index = lax.axis_index("pol")
    device_count, pols = lax.axis_size("fs"), lax.axis_size("pol")
    windows, all_coords = transform(facets[0], coords, device_count)
    parts = predict(windows, owners, counts, all_coords, device_index, facets.shape[1])
    visible = add_up(parts, pols)
    tables = jnp.concatenate(
        [
            lax.dynamic_slice_in_dim(jones_table, 4 * (pol_index // 2), 4, 0),
            lax.dynamic_slice_in_dim(jones_table, 4 * (pol_index % 2), 4, 0),
        ],
        axis=0,
    )
    return correct(visible, owners, counts, station_ids, tables, device_index)[None]


def solution(mesh):
    return jax.shard_map(
        on_device,
        mesh=mesh,
        in_specs=(
            P("pol", "fs", None, None),
            P(),
            P(),
            P(None, "fs", None, None),
            P("fs", None, None, None),
            P(),
        ),
        out_specs=P("pol", None, "fs", None, None),
        check_vma=False,
    )
```

```python
import functools
import math

import jax
import jax.numpy as jnp
import numpy as np
from jax import lax
from jax.experimental import pallas as pl
from jax.experimental.pallas import tpu as pltpu
from jax.sharding import PartitionSpec as P

R = 8
W = 64
S = 64
FH = 4096
SG = 512
LANES = 128
SPAN = 4
PITCH = 65
CHUNK = 2048
UNROLL = 32
PAIRS = 4
VMEM_BYTES = 67043328
SLACK = 13000 * 1024


def fit(values, terms):
    series = np.polynomial.chebyshev.Chebyshev.interpolate(
        lambda square: values(np.sqrt(np.maximum(square, 1e-12))), terms - 1, domain=[0.0, 0.25]
    )
    return [float(c) for c in series.convert(kind=np.polynomial.Polynomial).coef]


SIN_COEFS = fit(lambda r: np.sin(np.pi * r) / r, 5)
COS_COEFS = fit(lambda r: np.cos(np.pi * r), 5)


def unit_circle(turns):
    return np.exp(-2j * np.pi * turns)


def as_real(table):
    return np.concatenate(
        [
            np.concatenate([table.real, -table.imag], axis=-1),
            np.concatenate([table.imag, table.real], axis=-1),
        ],
        axis=-2,
    )


def mix_table():
    table = np.zeros((4 * W, 4 * W))
    col = np.arange(W)
    mirror = W - 1 - col
    a_real, a_imag, b_real, b_imag = mirror, W + mirror, 2 * W + col, 3 * W + col
    table[b_real, col] = table[a_real, col] = 1.0
    table[b_imag, W + col] = 1.0
    table[a_imag, W + col] = -1.0
    table[b_imag, 2 * W + col] = table[a_imag, 2 * W + col] = 1.0
    table[b_real, 3 * W + col] = -1.0
    table[a_real, 3 * W + col] = 1.0
    return table


def first_tables():
    n1 = np.arange(S)[:, None, None]
    k1 = np.arange(W)[None, :, None]
    n2 = np.arange(W)[None, None, :]
    rows = unit_circle((k1 * n2 % W) / W + (n1 * k1 % FH) / FH)
    upper, lower = rows[:, W // 2 :], rows[:, W // 2 - 1 :: -1]
    return as_real(np.concatenate([upper + lower, -1j * (upper - lower)], axis=1))


def second_table():
    index = np.arange(S)
    table = unit_circle((index[:, None] * index[None, :] % S) / S)
    return as_real(table) / (math.sqrt(FH) * SG)


def transform_tables():
    mix = mix_table().reshape(2, 2 * W, 2, 2 * W).transpose(0, 2, 1, 3).reshape(4, 2 * W, 2 * W)
    return np.concatenate([first_tables(), second_table()[None], mix])


def horner(coefs, square):
    total = jnp.full_like(square, coefs[-1])
    for coef in coefs[-2::-1]:
        total = total * square + coef
    return total


def phase(turns):
    rest = turns - jnp.round(turns)
    square = rest * rest
    half_cos = horner(COS_COEFS, square)
    half_sin = horner(SIN_COEFS, square) * rest
    double = half_sin + half_sin
    return 1.0 - double * half_sin, double * half_cos


def twice(left, right):
    return (left[0] * right[0] - left[1] * right[1], left[1] * right[0] + left[0] * right[1])


def chain(start, step, count):
    terms = [start, twice(start, step)]
    double = step[0] + step[0]
    while len(terms) < count:
        (last_cos, last_sin), (cos, sin) = terms[-2:]
        terms.append((double * cos - last_cos, double * sin - last_sin))
    return terms


def transform_kernel(
    device_count, strips_ref, tables_hbm, coords_ref, out_ref, gathered_ref,
    strip_ref, first_ref, mix_ref, second_ref, mixed_ref, turned_ref, everyone_ref, strip_sem, table_sem, own_sem,
    send_sem, recv_sem, pair_send_sem, pair_recv_sem
):
    me = lax.axis_index("fs")
    pol = lax.axis_index("pol")
    half = lax.rem(pol, 2)
    partner = {"pol": pol + 1 - 2 * half}
    facet_local = strip_ref.shape[0]
    slots = everyone_ref.shape[2] // 2
    span = min(SPAN, facet_local)
    pairs = span // 2

    order = []
    for group in range(facet_local // span):
        for pair in range(pairs):
            low = group * span + pairs - 1 - pair
            order.append((low, low + 2 * pair + 1))
    loads = [
        pltpu.make_async_copy(strips_ref.at[f], strip_ref.at[f], strip_sem.at[f])
        for f in range(facet_local)
    ]
    own = pltpu.make_async_copy(coords_ref, everyone_ref.at[me], own_sem)
    own.start()
    tables = [
        pltpu.make_async_copy(from_ref, to_ref, table_sem.at[i])
        for i, (from_ref, to_ref) in enumerate(
            [
                (tables_hbm.at[pl.ds(S + 1, 4)], mix_ref),
                (tables_hbm.at[pl.ds(0, S)], first_ref),
                (tables_hbm.at[S], second_ref),
            ]
        )
    ]
    tables[0].start()
    for i, (low, high) in enumerate(order):
        loads[low].start()
        loads[high].start()
        if i == 0:
            tables[1].start()
            tables[2].start()

    barrier = pltpu.get_barrier_semaphore()
    for step in range(1, device_count):
        pl.semaphore_signal(
            barrier,
            inc=1,
            device_id={"fs": lax.rem(me + step, device_count)},
            device_id_type=pl.DeviceIdType.MESH,
        )
    pl.semaphore_signal(barrier, inc=1, device_id=partner, device_id_type=pl.DeviceIdType.MESH)
    pl.semaphore_wait(barrier, device_count)
    own.wait()
    sends = []
    for step in range(1, device_count):
        mine = everyone_ref.at[me, :, pl.ds(half * slots, slots)]
        copy = pltpu.make_async_remote_copy(
            src_ref=mine,
            dst_ref=mine,
            send_sem=send_sem.at[step - 1],
            recv_sem=recv_sem.at[step - 1],
            device_id={"fs": lax.rem(me + step, device_count)},
            device_id_type=pl.DeviceIdType.MESH,
        )
        copy.start()
        sends.append(copy)

    tables[0].wait()
    mix = jnp.concatenate(
        [jnp.concatenate([mix_ref[2 * i], mix_ref[2 * i + 1]], axis=1) for i in range(2)], axis=0
    )

    def lanes(pieces):
        return jnp.concatenate(pieces, axis=1).astype(jnp.bfloat16)

    for group in range(facet_local // span):
        for pair in range(pairs):
            low, high = order[group * pairs + pair]
            loads[low].wait()
            loads[high].wait()

            def join(i, carry, low=low, high=high, pair=pair):
                rows = pl.ds(pl.multiple_of(i * CHUNK, CHUNK), CHUNK)
                both = jnp.dot(
                    jnp.concatenate([strip_ref[low, rows, :], strip_ref[high, rows, :]], axis=1),
                    mix,
                    preferred_element_type=jnp.float32,
                )
                for t in range(CHUNK // W):
                    to = pl.ds((i * (CHUNK // W) + t) * PITCH, W)
                    for part in range(2):
                        mixed_ref[2 * pair + part, to, :] = both[
                            W * t : W * (t + 1), LANES * part : LANES * (part + 1)
                        ]
                return carry

            lax.fori_loop(0, FH // CHUNK, join, 0)
        if group == 0:
            tables[1].wait()
            tables[2].wait()

        def put(to_ref, rows, product):
            for pair in range(pairs):
                for part in range(2):
                    to_ref[2 * pair + part, rows, :] = product[
                        W * part : W * (part + 1), LANES * pair : LANES * (pair + 1)
                    ]

        def take(from_ref, rows):
            return jnp.concatenate(
                [lanes([from_ref[2 * q + part, rows, :] for q in range(pairs)]) for part in range(2)],
                axis=0,
            )

        def first(i, carry):
            for u in range(UNROLL):
                rows = pl.ds(i * UNROLL + u, W, stride=PITCH)
                put(
                    turned_ref,
                    rows,
                    jnp.dot(
                        first_ref[i * UNROLL + u],
                        take(mixed_ref, rows),
                        preferred_element_type=jnp.float32,
                    ),
                )
            return carry

        lax.fori_loop(0, S // UNROLL, first, 0)

        def second(i, carry):
            for u in range(UNROLL):
                k = i * UNROLL + u
                put(
                    mixed_ref,
                    pl.ds(k, S, stride=PITCH),
                    jnp.dot(
                        second_ref[...],
                        take(turned_ref, pl.ds(k * PITCH, S)),
                        preferred_element_type=jnp.float32,
                    ),
                )
            return carry

        lax.fori_loop(0, W // UNROLL, second, 0)

        def third(i, carry, group=group):
            for u in range(2):
                s = i * 2 + u
                out_ref[s, pl.ds(group * 2 * W, 2 * W), :] = take(mixed_ref, pl.ds(s * PITCH, W))
            return carry

        lax.fori_loop(0, S // 2, third, 0)

    forwards = []
    for step in range(1, device_count):
        sends[step - 1].wait_recv()
        theirs = everyone_ref.at[
            lax.rem(me + device_count - step, device_count), :, pl.ds(half * slots, slots)
        ]
        copy = pltpu.make_async_remote_copy(
            src_ref=theirs,
            dst_ref=theirs,
            send_sem=pair_send_sem.at[step - 1],
            recv_sem=pair_recv_sem.at[step - 1],
            device_id=partner,
            device_id_type=pl.DeviceIdType.MESH,
        )
        copy.start()
        forwards.append(copy)
    for copy in forwards:
        copy.wait_recv()
    for copy in sends + forwards:
        copy.wait_send()
    gathered_ref[...] = everyone_ref[...]


def transform(strips, coords, device_count):
    vmem = pl.BlockSpec(memory_space=pltpu.VMEM)
    hbm = pl.BlockSpec(memory_space=pltpu.HBM)
    facet_local = strips.shape[0]
    span = min(SPAN, facet_local)
    scratch = pltpu.VMEM((span, S * PITCH, LANES), jnp.float32)
    kept = S * facet_local * 2 * W * W * 2 + device_count * coords.size * 4 + SLACK
    return pl.pallas_call(
        functools.partial(transform_kernel, device_count),
        out_shape=[
            jax.ShapeDtypeStruct((S, facet_local // span * 2 * W, span * W), jnp.bfloat16),
            jax.ShapeDtypeStruct((device_count,) + coords.shape, jnp.float32),
        ],
        in_specs=[hbm] * 3,
        out_specs=[vmem, vmem],
        scratch_shapes=[
            pltpu.VMEM((facet_local, FH, LANES), jnp.bfloat16),
            pltpu.VMEM((S, 2 * W, 2 * W), jnp.bfloat16),
            pltpu.VMEM((4, 2 * W, 2 * W), jnp.bfloat16),
            pltpu.VMEM((2 * S, 2 * S), jnp.bfloat16),
            scratch,
            scratch,
            pltpu.VMEM((device_count,) + coords.shape, jnp.float32),
            pltpu.SemaphoreType.DMA((facet_local,)),
            pltpu.SemaphoreType.DMA((3,)),
            pltpu.SemaphoreType.DMA,
            pltpu.SemaphoreType.DMA((device_count - 1,)),
            pltpu.SemaphoreType.DMA((device_count - 1,)),
            pltpu.SemaphoreType.DMA((device_count - 1,)),
            pltpu.SemaphoreType.DMA((device_count - 1,)),
        ],
        compiler_params=pltpu.CompilerParams(
            vmem_limit_bytes=VMEM_BYTES - kept, collective_id=0, has_side_effects=True
        ),
        cost_estimate=pl.CostEstimate(
            flops=5 * 10**9, bytes_accessed=16 * 2**20, transcendentals=0
        ),
    )(
        strips,
        pltpu.with_memory_space_constraint(jnp.asarray(transform_tables(), jnp.bfloat16), pltpu.HBM),
        pltpu.with_memory_space_constraint(coords, pltpu.HBM),
    )


def predict_kernel(
    facet_local, part, device_count, index_ref, owners_ref, counts_ref, coords_ref, windows_ref,
    *refs
):
    if part == 1:
        refs = refs[1:]
    limit_ref, *refs = refs
    parts_refs = refs[: device_count // 2]
    out_ref, table_ref, row_ref, list_ref, place_ref, load_ref, loads_ref = refs[device_count // 2 :]
    lane = out_ref.shape[3]
    near = device_count // 2
    subgrids = owners_ref.shape[0]
    capacity = parts_refs[0].shape[0]
    span = min(SPAN, facet_local)
    groups = facet_local // span
    steps = span // 2
    first = index_ref[0] * facet_local
    unit = 1.0 / SG
    row_middle = (lax.div(first, R) * W).astype(jnp.float32) + (0.5 * (W - 1) - SG // 2)
    col_middle = (lax.rem(first, R) * W).astype(jnp.float32) + (0.5 * (span * W - 1) - SG // 2)
    ramp = lax.broadcasted_iota(jnp.int32, (8, lane), 0).astype(jnp.float32)
    fine = (ramp + 0.5) * unit
    col_pick = jnp.where(ramp == 1.0, 0.0, col_middle + (ramp - 2.0) * (span * W))
    col_pick = jnp.where(ramp == 0.0, 8.0, col_pick) * unit
    row_pick = jnp.where(ramp == 0.0, 0.0, jnp.where(ramp == 1.0, 8.0, row_middle)) * unit
    out_ref[...] = jnp.zeros_like(out_ref)

    def clear(ref):
        def body(i, carry):
            ref[i] = 0
            return carry

        lax.fori_loop(0, ref.shape[0], body, 0)

    clear(loads_ref)
    clear(limit_ref)
    list_ref[0] = 0
    me = index_ref[0]

    def rank(s, carry):
        listed, total = carry
        owner = owners_ref[s]
        load = loads_ref[owner]
        loads_ref[owner] = load + 1
        count = counts_ref[s]
        offset = owner ^ me
        load_ref[s] = load
        place_ref[s] = (offset - (1 - part) * near) * capacity + load
        taken = jnp.where((offset >= near) == (part == 0), 1, 0)
        list_ref[listed] = s

        @pl.when(owner == me)
        def _():
            limit_ref[load] = count

        return listed + taken, total + taken * lax.div(count + 1, 2)

    listed, total = lax.fori_loop(0, subgrids, rank, (0, 0))
    last = jnp.maximum(listed - 1, 0)
    list_ref[listed] = list_ref[last]

    def following(i, b):
        items = []
        for _ in range(PAIRS):
            s = list_ref[i]
            items.append((s, b))
            done = b + 2 >= counts_ref[s]
            end = jnp.logical_and(done, i == last)
            b = jnp.where(end, b, jnp.where(done, 0, b + 2))
            i = jnp.where(done, jnp.minimum(i + 1, last), i)
        return items, (i, b)

    def tables(u, turn, s, b):
        owner, load = owners_ref[s], load_ref[s]
        for h in range(2):
            x = coords_ref[owner, 0, load, pl.ds(b + h, 1), :]
            y = coords_ref[owner, 1, load, pl.ds(b + h, 1), :]
            picked = phase(x * row_pick + y * col_pick)
            col_step, row_step = [
                [jnp.broadcast_to(part[i : i + 1], (8, lane)) for part in picked] for i in range(2)
            ]
            cols = chain(phase(y * fine), col_step, steps * W // 8)
            entries = []
            for k in range(steps):
                some = cols[W // 8 * k : W // 8 * (k + 1)]
                entries += [cos for cos, _ in some] + [sin for _, sin in some]
            table_ref[u, :, h * lane : (h + 1) * lane] = jnp.concatenate(entries, axis=0).astype(
                jnp.bfloat16
            )
            rows = chain(phase(x * fine), row_step, W // 16)
            row_ref[turn, u, h] = jnp.concatenate(
                [cos for cos, _ in rows] + [sin for _, sin in rows] + list(picked), axis=0
            )

    def predict(u, turn, s, b):
        grid = jnp.dot(windows_ref[s], table_ref[u], preferred_element_type=jnp.float32)
        place = place_ref[s]
        for h in range(2):
            real = imag = None
            for g in range(groups):
                sums = []
                for part in range(2):
                    total = None
                    for k in range(W // 8):
                        at = (2 * g + part) * W + 8 * k
                        term = grid[at : at + 8, h * lane : (h + 1) * lane] * row_ref[
                            turn, u, h, 8 * k : 8 * k + 8, :
                        ]
                        total = term if total is None else total + term
                    sums.append(total)
                cos = row_ref[turn, u, h, W + 2 + g : W + 3 + g, :]
                sin = row_ref[turn, u, h, W + 10 + g : W + 11 + g, :]
                more_real = sums[0] * cos + sums[1] * sin
                more_imag = sums[1] * cos - sums[0] * sin
                real = more_real if real is None else real + more_real
                imag = more_imag if imag is None else imag + more_imag
            out_ref[place, 0, pl.ds(b + h, 1), :] = jnp.sum(real, axis=0, keepdims=True)
            out_ref[place, 1, pl.ds(b + h, 1), :] = jnp.sum(imag, axis=0, keepdims=True)

    items, after = following(0, 0)
    for u, (s, b) in enumerate(items):
        tables(u, 0, s, b)

    def step(i, carry):
        items, after = carry
        for u, (s, b) in enumerate(items):
            predict(u, i & 1, s, b)
        items, after = following(*after)
        for u, (s, b) in enumerate(items):
            tables(u, (i + 1) & 1, s, b)
        return items, after

    lax.fori_loop(0, lax.div(total + PAIRS - 1, PAIRS), step, (items, after))
    for i, parts_ref in enumerate(parts_refs):
        parts_ref[...] = out_ref[i * capacity : (i + 1) * capacity].astype(jnp.bfloat16)


def predict(windows, owners, counts, coords, device_index, facet_local, before=()):
    device_count, _, capacity, max_blocks, lane = coords.shape
    smem = pl.BlockSpec(memory_space=pltpu.SMEM)
    vmem = pl.BlockSpec(memory_space=pltpu.VMEM)
    near = device_count // 2
    slots = (capacity, 2, max_blocks, lane)
    part = len(before)
    limit, *parts = pl.pallas_call(
        functools.partial(predict_kernel, facet_local, part, device_count),
        out_shape=[jax.ShapeDtypeStruct((capacity,), jnp.int32)]
        + [jax.ShapeDtypeStruct(slots, jnp.bfloat16)] * near,
        in_specs=[smem, smem, smem, vmem, vmem] + [smem] * part,
        out_specs=[smem] + [vmem] * near,
        scratch_shapes=[
            pltpu.VMEM((near * capacity,) + slots[1:], jnp.float32),
            pltpu.VMEM((PAIRS, windows.shape[2], 2 * lane), jnp.bfloat16),
            pltpu.VMEM((2, PAIRS, 2, W + 16, lane), jnp.float32),
            pltpu.SMEM((owners.shape[0] + 1,), jnp.int32),
            pltpu.SMEM((owners.shape[0],), jnp.int32),
            pltpu.SMEM((owners.shape[0],), jnp.int32),
            pltpu.SMEM((device_count,), jnp.int32),
        ],
        compiler_params=pltpu.CompilerParams(vmem_limit_bytes=16 * 2**20),
        cost_estimate=pl.CostEstimate(
            flops=2 * 10**10, bytes_accessed=2**20, transcendentals=0
        ),
    )(device_index.reshape(1), owners, counts, coords, windows, *before)
    return limit, parts


def flip(index, mask):
    bit = 1
    flipped = index
    while bit <= mask:
        if mask & bit:
            flipped = flipped + bit * (1 - 2 * lax.rem(lax.div(index, bit), 2))
        bit *= 2
    return flipped


def finish_kernel(near, pols, limit_ref, stations_hbm, table_ref, *refs):
    near_refs = refs[:near]
    far_refs = refs[near : 2 * near]
    (
        out_ref, far_ref, arrived_ref, station_ref, rows_ref, jones_ref, total_ref, sent_ref,
        far_sem, station_sem, send_sem, recv_sem, pol_send_sem, pol_recv_sem
    ) = refs[2 * near :]
    me = lax.axis_index("fs")
    pol = lax.axis_index("pol")
    capacity, _, max_blocks, lane = total_ref.shape
    peers = [{"fs": flip(me, mask)} for mask in range(1, near)]
    pol_peers = [{"pol": lax.rem(pol + step, pols)} for step in range(1, pols)]
    loads = [
        pltpu.make_async_copy(from_ref, far_ref.at[i], far_sem.at[i])
        for i, from_ref in enumerate(far_refs)
    ]
    stations = pltpu.make_async_copy(stations_hbm, station_ref, station_sem)
    for load in loads:
        load.start()
    stations.start()
    barrier = pltpu.get_barrier_semaphore()
    for peer in peers + pol_peers:
        pl.semaphore_signal(
            barrier, inc=1, device_id=peer, device_id_type=pl.DeviceIdType.MESH
        )
    pl.semaphore_wait(barrier, near + pols - 2)
    copies = []
    for i, peer in enumerate(peers):
        copy = pltpu.make_async_remote_copy(
            src_ref=near_refs[i + 1],
            dst_ref=arrived_ref.at[i],
            send_sem=send_sem.at[i],
            recv_sem=recv_sem.at[i],
            device_id=peer,
            device_id_type=pl.DeviceIdType.MESH,
        )
        copy.start()
        copies.append(copy)
    total = near_refs[0][...].astype(jnp.float32)
    for i, load in enumerate(loads):
        load.wait()
        total = total + far_ref[i].astype(jnp.float32)
    total_ref[...] = total
    for i, copy in enumerate(copies):
        copy.wait_recv()
        total_ref[...] += arrived_ref[i].astype(jnp.float32)
    sent_ref[pol] = total_ref[...].astype(jnp.bfloat16)
    pol_copies = []
    for i, peer in enumerate(pol_peers):
        copy = pltpu.make_async_remote_copy(
            src_ref=sent_ref.at[pol],
            dst_ref=sent_ref.at[pol],
            send_sem=pol_send_sem.at[i],
            recv_sem=pol_recv_sem.at[i],
            device_id=peer,
            device_id_type=pl.DeviceIdType.MESH,
        )
        copy.start()
        pol_copies.append(copy)
    stations.wait()
    chunks = table_ref.shape[1] // lane
    firsts = [4 * lax.div(pol, 2), 4 * lax.rem(pol, 2)]
    for row in range(table_ref.shape[0]):
        for chunk in range(chunks):
            at = row * chunks + chunk
            rows_ref[at : at + 1, :] = table_ref[row : row + 1, chunk * lane : (chunk + 1) * lane]

    def look_up(load, carry):
        for side in range(2):
            ids = station_ref[load, pl.ds(side, max_blocks, stride=2), :]
            low = ids & (lane - 1)
            high = ids >> (lane.bit_length() - 1)
            for row in range(4):
                entry = None
                for chunk in range(chunks):
                    source = jnp.broadcast_to(
                        rows_ref[pl.ds((firsts[side] + row) * chunks + chunk, 1), :],
                        (max_blocks, lane),
                    )
                    got = jnp.take_along_axis(source, low, axis=1, mode="promise_in_bounds")
                    entry = got if entry is None else jnp.where(high == chunk, got, entry)
                jones_ref[load, 4 * side + row] = entry
        return carry

    lax.fori_loop(0, capacity, look_up, 0)
    for copy in pol_copies:
        copy.wait_recv()
    block = lax.broadcasted_iota(jnp.int32, (max_blocks, lane), 0)

    def product(a, b):
        return (a[0] * b[0] - a[1] * b[1], a[0] * b[1] + a[1] * b[0])

    def correct(load, carry):
        jones = [jones_ref[load, i] for i in range(8)]
        real = jnp.zeros((max_blocks, lane), jnp.float32)
        imag = jnp.zeros((max_blocks, lane), jnp.float32)
        for row in range(2):
            for col in range(2):
                comp = 2 * row + col
                visible = [
                    jnp.where(
                        pol == comp, total_ref[load, i], sent_ref[comp, load, i].astype(jnp.float32)
                    )
                    for i in range(2)
                ]
                step = product((jones[2 * row], jones[2 * row + 1]), visible)
                step = product(step, (jones[4 + 2 * col], -jones[5 + 2 * col]))
                real = real + step[0]
                imag = imag + step[1]
        keep = block < limit_ref[load]
        out_ref[0, load] = jnp.where(keep, real, 0.0)
        out_ref[1, load] = jnp.where(keep, imag, 0.0)
        return carry

    lax.fori_loop(0, capacity, correct, 0)
    for copy in copies + pol_copies:
        copy.wait_send()


def finish(limit, near_parts, far_parts, station_ids, table, pols):
    near = len(near_parts)
    slots = near_parts[0].shape
    capacity, _, max_blocks, lane = slots
    smem = pl.BlockSpec(memory_space=pltpu.SMEM)
    vmem = pl.BlockSpec(memory_space=pltpu.VMEM)
    hbm = pl.BlockSpec(memory_space=pltpu.HBM)
    anywhere = pl.BlockSpec(memory_space=pl.ANY)
    return pl.pallas_call(
        functools.partial(finish_kernel, near, pols),
        out_shape=jax.ShapeDtypeStruct((2, capacity, max_blocks, lane), jnp.float32),
        in_specs=[smem, hbm, vmem] + [vmem] * near + [anywhere] * near,
        out_specs=vmem,
        scratch_shapes=[
            pltpu.VMEM((near,) + slots, jnp.bfloat16),
            pltpu.VMEM((near - 1,) + slots, jnp.bfloat16),
            pltpu.VMEM((capacity, 2 * max_blocks, lane), jnp.int32),
            pltpu.VMEM((table.size // lane, lane), jnp.float32),
            pltpu.VMEM((capacity, 8, max_blocks, lane), jnp.float32),
            pltpu.VMEM(slots, jnp.float32),
            pltpu.VMEM((pols,) + slots, jnp.bfloat16),
            pltpu.SemaphoreType.DMA((near,)),
            pltpu.SemaphoreType.DMA,
            pltpu.SemaphoreType.DMA((near - 1,)),
            pltpu.SemaphoreType.DMA((near - 1,)),
            pltpu.SemaphoreType.DMA((pols - 1,)),
            pltpu.SemaphoreType.DMA((pols - 1,)),
        ],
        compiler_params=pltpu.CompilerParams(
            vmem_limit_bytes=8 * 2**20, collective_id=1, has_side_effects=True
        ),
    )(
        limit,
        station_ids.reshape(capacity, 2 * max_blocks, lane),
        table,
        *near_parts,
        *far_parts,
    )


def on_device(facets, owners, counts, coords, station_ids, jones_table):
    device_index = lax.axis_index("fs").astype(jnp.int32)
    device_count, pols = lax.axis_size("fs"), lax.axis_size("pol")
    windows, all_coords = transform(facets[0], coords, device_count)
    near = device_count // 2
    first, parts = predict(windows, owners, counts, all_coords, device_index, facets.shape[1])
    far_parts = [
        lax.ppermute(part, "fs", [(i, i ^ (near + mask)) for i in range(device_count)])
        for mask, part in enumerate(parts)
    ]
    limit, near_parts = predict(
        windows, owners, counts, all_coords, device_index, facets.shape[1], (first,)
    )
    return finish(limit, near_parts, far_parts, station_ids, jones_table, pols)[None]


def solution(mesh):
    return jax.shard_map(
        on_device,
        mesh=mesh,
        in_specs=(
            P("pol", "fs", None, None),
            P(),
            P(),
            P(None, "fs", None, None),
            P("fs", None, None, None),
            P(),
        ),
        out_specs=P("pol", None, "fs", None, None),
        check_vma=False,
    )
```

```python
import functools
import math

import jax
import jax.numpy as jnp
import numpy as np
from jax import lax
from jax.experimental import pallas as pl
from jax.experimental.pallas import tpu as pltpu
from jax.sharding import PartitionSpec as P

R = 8
W = 64
S = 64
FH = 4096
SG = 512
LANES = 128
SPAN = 4
PITCH = 65
CHUNK = 2048
UNROLL = 32
PAIRS = 4
VMEM_BYTES = 67043328
SLACK = 13000 * 1024


def fit(values, terms):
    series = np.polynomial.chebyshev.Chebyshev.interpolate(
        lambda square: values(np.sqrt(np.maximum(square, 1e-12))), terms - 1, domain=[0.0, 0.25]
    )
    return [float(c) for c in series.convert(kind=np.polynomial.Polynomial).coef]


SIN_COEFS = fit(lambda r: np.sin(np.pi * r) / r, 5)
COS_COEFS = fit(lambda r: np.cos(np.pi * r), 5)


def unit_circle(turns):
    return np.exp(-2j * np.pi * turns)


def as_real(table):
    return np.concatenate(
        [
            np.concatenate([table.real, -table.imag], axis=-1),
            np.concatenate([table.imag, table.real], axis=-1),
        ],
        axis=-2,
    )


def mix_table():
    table = np.zeros((4 * W, 4 * W))
    col = np.arange(W)
    mirror = W - 1 - col
    a_real, a_imag, b_real, b_imag = mirror, W + mirror, 2 * W + col, 3 * W + col
    table[b_real, col] = table[a_real, col] = 1.0
    table[b_imag, W + col] = 1.0
    table[a_imag, W + col] = -1.0
    table[b_imag, 2 * W + col] = table[a_imag, 2 * W + col] = 1.0
    table[b_real, 3 * W + col] = -1.0
    table[a_real, 3 * W + col] = 1.0
    return table


def first_tables():
    n1 = np.arange(S)[:, None, None]
    k1 = np.arange(W)[None, :, None]
    n2 = np.arange(W)[None, None, :]
    rows = unit_circle((k1 * n2 % W) / W + (n1 * k1 % FH) / FH)
    upper, lower = rows[:, W // 2 :], rows[:, W // 2 - 1 :: -1]
    return as_real(np.concatenate([upper + lower, -1j * (upper - lower)], axis=1))


def second_table():
    index = np.arange(S)
    table = unit_circle((index[:, None] * index[None, :] % S) / S)
    return as_real(table) / (math.sqrt(FH) * SG)


def transform_tables():
    mix = mix_table().reshape(2, 2 * W, 2, 2 * W).transpose(0, 2, 1, 3).reshape(4, 2 * W, 2 * W)
    return np.concatenate([first_tables(), second_table()[None], mix])


def horner(coefs, square):
    total = jnp.full_like(square, coefs[-1])
    for coef in coefs[-2::-1]:
        total = total * square + coef
    return total


def phase(turns):
    rest = turns - jnp.round(turns)
    square = rest * rest
    half_cos = horner(COS_COEFS, square)
    half_sin = horner(SIN_COEFS, square) * rest
    double = half_sin + half_sin
    return 1.0 - double * half_sin, double * half_cos


def twice(left, right):
    return (left[0] * right[0] - left[1] * right[1], left[1] * right[0] + left[0] * right[1])


def chain(start, step, count):
    terms = [start, twice(start, step)]
    double = step[0] + step[0]
    while len(terms) < count:
        (last_cos, last_sin), (cos, sin) = terms[-2:]
        terms.append((double * cos - last_cos, double * sin - last_sin))
    return terms


def flip(index, mask):
    bit = 1
    flipped = index
    while bit <= mask:
        if mask & bit:
            flipped = flipped + bit * (1 - 2 * lax.rem(lax.div(index, bit), 2))
        bit *= 2
    return flipped


def transform_kernel(
    device_count, strips_ref, tables_hbm, coords_ref, out_ref, gathered_ref,
    strip_ref, first_ref, mix_ref, second_ref, mixed_ref, turned_ref, everyone_ref, strip_sem, table_sem, own_sem,
    pair_send_sem, pair_recv_sem, line_send_sem, line_recv_sem, core_send_sem, core_recv_sem
):
    me = lax.axis_index("fs")
    pol = lax.axis_index("pol")
    half = lax.rem(pol, 2)
    partner = {"pol": pol + 1 - 2 * half}
    facet_local = strip_ref.shape[0]
    slots = everyone_ref.shape[2] // 2
    span = min(SPAN, facet_local)
    pairs = span // 2

    order = []
    for group in range(facet_local // span):
        for pair in range(pairs):
            low = group * span + pairs - 1 - pair
            order.append((low, low + 2 * pair + 1))
    loads = [
        pltpu.make_async_copy(strips_ref.at[f], strip_ref.at[f], strip_sem.at[f])
        for f in range(facet_local)
    ]
    own = pltpu.make_async_copy(coords_ref, everyone_ref.at[me], own_sem)
    own.start()
    tables = [
        pltpu.make_async_copy(from_ref, to_ref, table_sem.at[i])
        for i, (from_ref, to_ref) in enumerate(
            [
                (tables_hbm.at[pl.ds(S + 1, 4)], mix_ref),
                (tables_hbm.at[pl.ds(0, S)], first_ref),
                (tables_hbm.at[S], second_ref),
            ]
        )
    ]
    tables[0].start()
    for i, (low, high) in enumerate(order):
        loads[low].start()
        loads[high].start()
        if i == 0:
            tables[1].start()
            tables[2].start()

    across = {"fs": flip(me, 1)}
    line = {h: {"fs": flip(me, 2 * h)} for h in range(1, device_count // 2)}
    barrier = pltpu.get_barrier_semaphore()
    for peer in [partner, across] + list(line.values()):
        pl.semaphore_signal(barrier, inc=1, device_id=peer, device_id_type=pl.DeviceIdType.MESH)
    pl.semaphore_wait(barrier, device_count // 2 + 1)
    own.wait()
    sends = []

    def send(source, peer, send_sem, recv_sem, index):
        piece = everyone_ref.at[source, :, pl.ds(half * slots, slots)]
        copy = pltpu.make_async_remote_copy(
            src_ref=piece,
            dst_ref=piece,
            send_sem=send_sem.at[index],
            recv_sem=recv_sem.at[index],
            device_id=peer,
            device_id_type=pl.DeviceIdType.MESH,
        )
        copy.start()
        sends.append(copy)
        return copy

    def to_partner(mask):
        return send(flip(me, mask), partner, core_send_sem, core_recv_sem, mask - 1)

    crossed = {0: send(me, across, pair_send_sem, pair_recv_sem, 0)}
    reached = {
        h: send(me, line[h], line_send_sem, line_recv_sem, h - 1) for h in reversed(list(line))
    }
    handed = []

    def relay(masks):
        for h in masks:
            reached[h].wait_recv()
            crossed[h] = send(flip(me, 2 * h), across, pair_send_sem, pair_recv_sem, h)
            handed.append(to_partner(2 * h))

    tables[0].wait()
    mix = jnp.concatenate(
        [jnp.concatenate([mix_ref[2 * i], mix_ref[2 * i + 1]], axis=1) for i in range(2)], axis=0
    )

    def lanes(pieces):
        return jnp.concatenate(pieces, axis=1).astype(jnp.bfloat16)

    for group in range(facet_local // span):
        for pair in range(pairs):
            low, high = order[group * pairs + pair]
            loads[low].wait()
            loads[high].wait()

            def join(i, carry, low=low, high=high, pair=pair):
                rows = pl.ds(pl.multiple_of(i * CHUNK, CHUNK), CHUNK)
                both = jnp.dot(
                    jnp.concatenate([strip_ref[low, rows, :], strip_ref[high, rows, :]], axis=1),
                    mix,
                    preferred_element_type=jnp.float32,
                )
                for t in range(CHUNK // W):
                    to = pl.ds((i * (CHUNK // W) + t) * PITCH, W)
                    for part in range(2):
                        mixed_ref[2 * pair + part, to, :] = both[
                            W * t : W * (t + 1), LANES * part : LANES * (part + 1)
                        ]
                return carry

            lax.fori_loop(0, FH // CHUNK, join, 0)
        if group == 0:
            tables[1].wait()
            tables[2].wait()

        def put(to_ref, rows, product):
            for pair in range(pairs):
                for part in range(2):
                    to_ref[2 * pair + part, rows, :] = product[
                        W * part : W * (part + 1), LANES * pair : LANES * (pair + 1)
                    ]

        def take(from_ref, rows):
            return jnp.concatenate(
                [lanes([from_ref[2 * q + part, rows, :] for q in range(pairs)]) for part in range(2)],
                axis=0,
            )

        def first(i, carry):
            for u in range(UNROLL):
                rows = pl.ds(i * UNROLL + u, W, stride=PITCH)
                put(
                    turned_ref,
                    rows,
                    jnp.dot(
                        first_ref[i * UNROLL + u],
                        take(mixed_ref, rows),
                        preferred_element_type=jnp.float32,
                    ),
                )
            return carry

        lax.fori_loop(0, S // UNROLL, first, 0)
        if group == 0:
            relay([1])

        def second(i, carry):
            for u in range(UNROLL):
                k = i * UNROLL + u
                put(
                    mixed_ref,
                    pl.ds(k, S, stride=PITCH),
                    jnp.dot(
                        second_ref[...],
                        take(turned_ref, pl.ds(k * PITCH, S)),
                        preferred_element_type=jnp.float32,
                    ),
                )
            return carry

        lax.fori_loop(0, W // UNROLL, second, 0)
        if group == 0:
            relay(range(2, device_count // 2))

        def third(i, carry, group=group):
            for u in range(2):
                s = i * 2 + u
                out_ref[s, pl.ds(group * 2 * W, 2 * W), :] = take(mixed_ref, pl.ds(s * PITCH, W))
            return carry

        lax.fori_loop(0, S // 2, third, 0)

    for h in range(device_count // 2):
        crossed[h].wait_recv()
        handed.append(to_partner(2 * h + 1))
    for copy in handed:
        copy.wait_recv()
    for copy in sends:
        copy.wait_send()
    gathered_ref[...] = everyone_ref[...]


def transform(strips, coords, device_count):
    vmem = pl.BlockSpec(memory_space=pltpu.VMEM)
    hbm = pl.BlockSpec(memory_space=pltpu.HBM)
    facet_local = strips.shape[0]
    span = min(SPAN, facet_local)
    scratch = pltpu.VMEM((span, S * PITCH, LANES), jnp.float32)
    kept = S * facet_local * 2 * W * W * 2 + device_count * coords.size * 4 + SLACK
    return pl.pallas_call(
        functools.partial(transform_kernel, device_count),
        out_shape=[
            jax.ShapeDtypeStruct((S, facet_local // span * 2 * W, span * W), jnp.bfloat16),
            jax.ShapeDtypeStruct((device_count,) + coords.shape, jnp.float32),
        ],
        in_specs=[hbm] * 3,
        out_specs=[vmem, vmem],
        scratch_shapes=[
            pltpu.VMEM((facet_local, FH, LANES), jnp.bfloat16),
            pltpu.VMEM((S, 2 * W, 2 * W), jnp.bfloat16),
            pltpu.VMEM((4, 2 * W, 2 * W), jnp.bfloat16),
            pltpu.VMEM((2 * S, 2 * S), jnp.bfloat16),
            scratch,
            scratch,
            pltpu.VMEM((device_count,) + coords.shape, jnp.float32),
            pltpu.SemaphoreType.DMA((facet_local,)),
            pltpu.SemaphoreType.DMA((3,)),
            pltpu.SemaphoreType.DMA,
            pltpu.SemaphoreType.DMA((device_count // 2,)),
            pltpu.SemaphoreType.DMA((device_count // 2,)),
            pltpu.SemaphoreType.DMA((device_count // 2 - 1,)),
            pltpu.SemaphoreType.DMA((device_count // 2 - 1,)),
            pltpu.SemaphoreType.DMA((device_count - 1,)),
            pltpu.SemaphoreType.DMA((device_count - 1,)),
        ],
        compiler_params=pltpu.CompilerParams(
            vmem_limit_bytes=VMEM_BYTES - kept, collective_id=0, has_side_effects=True
        ),
        cost_estimate=pl.CostEstimate(
            flops=5 * 10**9, bytes_accessed=16 * 2**20, transcendentals=0
        ),
    )(
        strips,
        pltpu.with_memory_space_constraint(jnp.asarray(transform_tables(), jnp.bfloat16), pltpu.HBM),
        pltpu.with_memory_space_constraint(coords, pltpu.HBM),
    )


def predict_kernel(
    facet_local, device_count, index_ref, owners_ref, counts_ref, coords_ref, windows_ref,
    limit_ref, kept_ref, sent_ref, out_ref, table_ref, row_ref, place_ref, load_ref, loads_ref
):
    lane = out_ref.shape[3]
    half = device_count // 2
    subgrids = owners_ref.shape[0]
    capacity = kept_ref.shape[1]
    span = min(SPAN, facet_local)
    groups = facet_local // span
    steps = span // 2
    first = index_ref[0] * facet_local
    unit = 1.0 / SG
    row_middle = (lax.div(first, R) * W).astype(jnp.float32) + (0.5 * (W - 1) - SG // 2)
    col_middle = (lax.rem(first, R) * W).astype(jnp.float32) + (0.5 * (span * W - 1) - SG // 2)
    ramp = lax.broadcasted_iota(jnp.int32, (8, lane), 0).astype(jnp.float32)
    fine = (ramp + 0.5) * unit
    col_pick = jnp.where(ramp == 1.0, 0.0, col_middle + (ramp - 2.0) * (span * W))
    col_pick = jnp.where(ramp == 0.0, 8.0, col_pick) * unit
    row_pick = jnp.where(ramp == 0.0, 0.0, jnp.where(ramp == 1.0, 8.0, row_middle)) * unit
    out_ref[...] = jnp.zeros_like(out_ref)

    def clear(ref):
        def body(i, carry):
            ref[i] = 0
            return carry

        lax.fori_loop(0, ref.shape[0], body, 0)

    clear(loads_ref)
    clear(limit_ref)
    me = index_ref[0]

    def rank(s, total):
        owner = owners_ref[s]
        load = loads_ref[owner]
        loads_ref[owner] = load + 1
        count = counts_ref[s]
        offset = owner ^ me
        load_ref[s] = load
        place_ref[s] = ((offset & 1) * half + (offset >> 1)) * capacity + load

        @pl.when(owner == me)
        def _():
            limit_ref[load] = count

        return total + lax.div(count + 1, 2)

    total = lax.fori_loop(0, subgrids, rank, 0)

    def following(s, b):
        items = []
        for _ in range(PAIRS):
            items.append((s, b))
            done = b + 2 >= counts_ref[s]
            end = jnp.logical_and(done, s == subgrids - 1)
            b = jnp.where(end, b, jnp.where(done, 0, b + 2))
            s = jnp.where(done, jnp.minimum(s + 1, subgrids - 1), s)
        return items, (s, b)

    def tables(u, turn, s, b):
        owner, load = owners_ref[s], load_ref[s]
        for h in range(2):
            x = coords_ref[owner, 0, load, pl.ds(b + h, 1), :]
            y = coords_ref[owner, 1, load, pl.ds(b + h, 1), :]
            picked = phase(x * row_pick + y * col_pick)
            col_step, row_step = [
                [jnp.broadcast_to(part[i : i + 1], (8, lane)) for part in picked] for i in range(2)
            ]
            cols = chain(phase(y * fine), col_step, steps * W // 8)
            entries = []
            for k in range(steps):
                some = cols[W // 8 * k : W // 8 * (k + 1)]
                entries += [cos for cos, _ in some] + [sin for _, sin in some]
            table_ref[u, :, h * lane : (h + 1) * lane] = jnp.concatenate(entries, axis=0).astype(
                jnp.bfloat16
            )
            rows = chain(phase(x * fine), row_step, W // 16)
            row_ref[turn, u, h] = jnp.concatenate(
                [cos for cos, _ in rows] + [sin for _, sin in rows] + list(picked), axis=0
            )

    def predict(u, turn, s, b):
        grid = jnp.dot(windows_ref[s], table_ref[u], preferred_element_type=jnp.float32)
        place = place_ref[s]
        for h in range(2):
            real = imag = None
            for g in range(groups):
                sums = []
                for part in range(2):
                    total = None
                    for k in range(W // 8):
                        at = (2 * g + part) * W + 8 * k
                        term = grid[at : at + 8, h * lane : (h + 1) * lane] * row_ref[
                            turn, u, h, 8 * k : 8 * k + 8, :
                        ]
                        total = term if total is None else total + term
                    sums.append(total)
                cos = row_ref[turn, u, h, W + 2 + g : W + 3 + g, :]
                sin = row_ref[turn, u, h, W + 10 + g : W + 11 + g, :]
                more_real = sums[0] * cos + sums[1] * sin
                more_imag = sums[1] * cos - sums[0] * sin
                real = more_real if real is None else real + more_real
                imag = more_imag if imag is None else imag + more_imag
            out_ref[place, 0, pl.ds(b + h, 1), :] = jnp.sum(real, axis=0, keepdims=True)
            out_ref[place, 1, pl.ds(b + h, 1), :] = jnp.sum(imag, axis=0, keepdims=True)

    items, after = following(0, 0)
    for u, (s, b) in enumerate(items):
        tables(u, 0, s, b)

    def step(i, carry):
        items, after = carry
        for u, (s, b) in enumerate(items):
            predict(u, i & 1, s, b)
        items, after = following(*after)
        for u, (s, b) in enumerate(items):
            tables(u, (i + 1) & 1, s, b)
        return items, after

    lax.fori_loop(0, lax.div(total + PAIRS - 1, PAIRS), step, (items, after))
    kept_ref[...] = out_ref[: half * capacity].reshape(kept_ref.shape)
    sent_ref[...] = out_ref[half * capacity :].reshape(sent_ref.shape).astype(jnp.bfloat16)


def predict(windows, owners, counts, coords, device_index, facet_local):
    device_count, _, capacity, max_blocks, lane = coords.shape
    smem = pl.BlockSpec(memory_space=pltpu.SMEM)
    vmem = pl.BlockSpec(memory_space=pltpu.VMEM)
    slots = (capacity, 2, max_blocks, lane)
    half = (device_count // 2,) + slots
    return pl.pallas_call(
        functools.partial(predict_kernel, facet_local, device_count),
        out_shape=[
            jax.ShapeDtypeStruct((capacity,), jnp.int32),
            jax.ShapeDtypeStruct(half, jnp.float32),
            jax.ShapeDtypeStruct(half, jnp.bfloat16),
        ],
        in_specs=[smem, smem, smem, vmem, vmem],
        out_specs=[smem, vmem, vmem],
        scratch_shapes=[
            pltpu.VMEM((device_count * capacity,) + slots[1:], jnp.float32),
            pltpu.VMEM((PAIRS, windows.shape[2], 2 * lane), jnp.bfloat16),
            pltpu.VMEM((2, PAIRS, 2, W + 16, lane), jnp.float32),
            pltpu.SMEM((owners.shape[0],), jnp.int32),
            pltpu.SMEM((owners.shape[0],), jnp.int32),
            pltpu.SMEM((device_count,), jnp.int32),
        ],
        compiler_params=pltpu.CompilerParams(vmem_limit_bytes=16 * 2**20),
        cost_estimate=pl.CostEstimate(
            flops=2 * 10**10, bytes_accessed=2**20, transcendentals=0
        ),
    )(device_index.reshape(1), owners, counts, coords, windows)


def finish_kernel(
    half, pols, limit_ref, stations_hbm, table_ref, kept_ref, cross_ref, out_ref, pair_ref, line_ref,
    partial_ref, station_ref, rows_ref, jones_ref, total_ref, sent_ref, station_sem, pair_send_sem,
    pair_recv_sem, line_send_sem, line_recv_sem, pol_send_sem, pol_recv_sem
):
    me = lax.axis_index("fs")
    pol = lax.axis_index("pol")
    capacity, _, max_blocks, lane = total_ref.shape
    pair = {"fs": flip(me, 1)}
    line = [{"fs": flip(me, 2 * h)} for h in range(1, half)]
    pol_peers = [{"pol": lax.rem(pol + step, pols)} for step in range(1, pols)]
    stations = pltpu.make_async_copy(stations_hbm, station_ref, station_sem)
    stations.start()
    barrier = pltpu.get_barrier_semaphore()
    for peer in [pair] + line + pol_peers:
        pl.semaphore_signal(
            barrier, inc=1, device_id=peer, device_id_type=pl.DeviceIdType.MESH
        )
    pl.semaphore_wait(barrier, half + pols - 1)
    crossing = []
    for h in reversed(range(half)):
        copy = pltpu.make_async_remote_copy(
            src_ref=cross_ref.at[h],
            dst_ref=pair_ref.at[h],
            send_sem=pair_send_sem.at[h],
            recv_sem=pair_recv_sem.at[h],
            device_id=pair,
            device_id_type=pl.DeviceIdType.MESH,
        )
        copy.start()
        crossing.append(copy)
    copies = []
    for i, h in enumerate(reversed(range(1, half))):
        crossing[i].wait_recv()
        partial_ref[h - 1] = (kept_ref[h] + pair_ref[h].astype(jnp.float32)).astype(jnp.bfloat16)
        copy = pltpu.make_async_remote_copy(
            src_ref=partial_ref.at[h - 1],
            dst_ref=line_ref.at[h - 1],
            send_sem=line_send_sem.at[h - 1],
            recv_sem=line_recv_sem.at[h - 1],
            device_id=line[h - 1],
            device_id_type=pl.DeviceIdType.MESH,
        )
        copy.start()
        copies.append(copy)
    crossing[-1].wait_recv()
    total_ref[...] = kept_ref[0] + pair_ref[0].astype(jnp.float32)
    for copy in copies:
        copy.wait_recv()
    total = total_ref[...]
    for h in range(1, half):
        total = total + line_ref[h - 1].astype(jnp.float32)
    total_ref[...] = total
    sent_ref[pol] = total.astype(jnp.bfloat16)
    pol_copies = []
    for i, peer in enumerate(pol_peers):
        copy = pltpu.make_async_remote_copy(
            src_ref=sent_ref.at[pol],
            dst_ref=sent_ref.at[pol],
            send_sem=pol_send_sem.at[i],
            recv_sem=pol_recv_sem.at[i],
            device_id=peer,
            device_id_type=pl.DeviceIdType.MESH,
        )
        copy.start()
        pol_copies.append(copy)
    stations.wait()
    chunks = table_ref.shape[1] // lane
    firsts = [4 * lax.div(pol, 2), 4 * lax.rem(pol, 2)]
    for row in range(table_ref.shape[0]):
        for chunk in range(chunks):
            at = row * chunks + chunk
            rows_ref[at : at + 1, :] = table_ref[row : row + 1, chunk * lane : (chunk + 1) * lane]

    def look_up(load, carry):
        for side in range(2):
            ids = station_ref[load, pl.ds(side, max_blocks, stride=2), :]
            low = ids & (lane - 1)
            high = ids >> (lane.bit_length() - 1)
            for row in range(4):
                entry = None
                for chunk in range(chunks):
                    source = jnp.broadcast_to(
                        rows_ref[pl.ds((firsts[side] + row) * chunks + chunk, 1), :],
                        (max_blocks, lane),
                    )
                    got = jnp.take_along_axis(source, low, axis=1, mode="promise_in_bounds")
                    entry = got if entry is None else jnp.where(high == chunk, got, entry)
                jones_ref[load, 4 * side + row] = entry
        return carry

    lax.fori_loop(0, capacity, look_up, 0)
    for copy in pol_copies:
        copy.wait_recv()
    block = lax.broadcasted_iota(jnp.int32, (max_blocks, lane), 0)

    def product(a, b):
        return (a[0] * b[0] - a[1] * b[1], a[0] * b[1] + a[1] * b[0])

    def correct(load, carry):
        jones = [jones_ref[load, i] for i in range(8)]
        real = jnp.zeros((max_blocks, lane), jnp.float32)
        imag = jnp.zeros((max_blocks, lane), jnp.float32)
        for row in range(2):
            for col in range(2):
                comp = 2 * row + col
                visible = [
                    jnp.where(
                        pol == comp, total_ref[load, i], sent_ref[comp, load, i].astype(jnp.float32)
                    )
                    for i in range(2)
                ]
                step = product((jones[2 * row], jones[2 * row + 1]), visible)
                step = product(step, (jones[4 + 2 * col], -jones[5 + 2 * col]))
                real = real + step[0]
                imag = imag + step[1]
        keep = block < limit_ref[load]
        out_ref[0, load] = jnp.where(keep, real, 0.0)
        out_ref[1, load] = jnp.where(keep, imag, 0.0)
        return carry

    lax.fori_loop(0, capacity, correct, 0)
    for copy in crossing + copies + pol_copies:
        copy.wait_send()


def finish(limit, kept, sent, station_ids, table, pols):
    half = kept.shape[0]
    slots = kept.shape[1:]
    capacity, _, max_blocks, lane = slots
    smem = pl.BlockSpec(memory_space=pltpu.SMEM)
    vmem = pl.BlockSpec(memory_space=pltpu.VMEM)
    hbm = pl.BlockSpec(memory_space=pltpu.HBM)
    return pl.pallas_call(
        functools.partial(finish_kernel, half, pols),
        out_shape=jax.ShapeDtypeStruct((2, capacity, max_blocks, lane), jnp.float32),
        in_specs=[smem, hbm, vmem, vmem, vmem],
        out_specs=vmem,
        scratch_shapes=[
            pltpu.VMEM((half,) + slots, jnp.bfloat16),
            pltpu.VMEM((half - 1,) + slots, jnp.bfloat16),
            pltpu.VMEM((half - 1,) + slots, jnp.bfloat16),
            pltpu.VMEM((capacity, 2 * max_blocks, lane), jnp.int32),
            pltpu.VMEM((table.size // lane, lane), jnp.float32),
            pltpu.VMEM((capacity, 8, max_blocks, lane), jnp.float32),
            pltpu.VMEM(slots, jnp.float32),
            pltpu.VMEM((pols,) + slots, jnp.bfloat16),
            pltpu.SemaphoreType.DMA,
            pltpu.SemaphoreType.DMA((half,)),
            pltpu.SemaphoreType.DMA((half,)),
            pltpu.SemaphoreType.DMA((half - 1,)),
            pltpu.SemaphoreType.DMA((half - 1,)),
            pltpu.SemaphoreType.DMA((pols - 1,)),
            pltpu.SemaphoreType.DMA((pols - 1,)),
        ],
        compiler_params=pltpu.CompilerParams(
            vmem_limit_bytes=8 * 2**20, collective_id=1, has_side_effects=True
        ),
    )(
        limit,
        pltpu.with_memory_space_constraint(
            station_ids.reshape(capacity, 2 * max_blocks, lane), pltpu.HBM
        ),
        table,
        kept,
        sent,
    )


def on_device(facets, owners, counts, coords, station_ids, jones_table):
    device_index = lax.axis_index("fs").astype(jnp.int32)
    device_count, pols = lax.axis_size("fs"), lax.axis_size("pol")
    windows, all_coords = transform(facets[0], coords, device_count)
    limit, kept, sent = predict(
        windows, owners, counts, all_coords, device_index, facets.shape[1]
    )
    return finish(limit, kept, sent, station_ids, jones_table, pols)[None]


def solution(mesh):
    return jax.shard_map(
        on_device,
        mesh=mesh,
        in_specs=(
            P("pol", "fs", None, None),
            P(),
            P(),
            P(None, "fs", None, None),
            P("fs", None, None, None),
            P(),
        ),
        out_specs=P("pol", None, "fs", None, None),
        check_vma=False,
    )
```

```python
import functools
import math

import jax
import jax.numpy as jnp
import numpy as np
from jax import lax
from jax.experimental import pallas as pl
from jax.experimental.pallas import tpu as pltpu
from jax.sharding import PartitionSpec as P

R = 8
W = 64
S = 64
FH = 4096
SG = 512
LANES = 128
SPAN = 4
PITCH = 65
CHUNK = 2048
UNROLL = 32
PAIRS = 3
VMEM_BYTES = 67043328
SLACK = 13000 * 1024


def fit(values, terms):
    series = np.polynomial.chebyshev.Chebyshev.interpolate(
        lambda square: values(np.sqrt(np.maximum(square, 1e-12))), terms - 1, domain=[0.0, 0.25]
    )
    return [float(c) for c in series.convert(kind=np.polynomial.Polynomial).coef]


SIN_COEFS = fit(lambda r: np.sin(np.pi * r) / r, 5)
COS_COEFS = fit(lambda r: np.cos(np.pi * r), 5)


def unit_circle(turns):
    return np.exp(-2j * np.pi * turns)


def as_real(table):
    return np.concatenate(
        [
            np.concatenate([table.real, -table.imag], axis=-1),
            np.concatenate([table.imag, table.real], axis=-1),
        ],
        axis=-2,
    )


def mix_table():
    table = np.zeros((4 * W, 4 * W))
    col = np.arange(W)
    mirror = W - 1 - col
    a_real, a_imag, b_real, b_imag = mirror, W + mirror, 2 * W + col, 3 * W + col
    table[b_real, col] = table[a_real, col] = 1.0
    table[b_imag, W + col] = 1.0
    table[a_imag, W + col] = -1.0
    table[b_imag, 2 * W + col] = table[a_imag, 2 * W + col] = 1.0
    table[b_real, 3 * W + col] = -1.0
    table[a_real, 3 * W + col] = 1.0
    return table


def first_tables():
    n1 = np.arange(S)[:, None, None]
    k1 = np.arange(W)[None, :, None]
    n2 = np.arange(W)[None, None, :]
    rows = unit_circle((k1 * n2 % W) / W + (n1 * k1 % FH) / FH)
    upper, lower = rows[:, W // 2 :], rows[:, W // 2 - 1 :: -1]
    return as_real(np.concatenate([upper + lower, -1j * (upper - lower)], axis=1))


def second_table():
    index = np.arange(S)
    table = unit_circle((index[:, None] * index[None, :] % S) / S)
    return as_real(table) / (math.sqrt(FH) * SG)


def transform_tables():
    mix = mix_table().reshape(2, 2 * W, 2, 2 * W).transpose(0, 2, 1, 3).reshape(4, 2 * W, 2 * W)
    return np.concatenate([first_tables(), second_table()[None], mix])


def horner(coefs, square):
    total = jnp.full_like(square, coefs[-1])
    for coef in coefs[-2::-1]:
        total = total * square + coef
    return total


def phase(turns):
    rest = turns - jnp.round(turns)
    square = rest * rest
    half_cos = horner(COS_COEFS, square)
    half_sin = horner(SIN_COEFS, square) * rest
    double = half_sin + half_sin
    return 1.0 - double * half_sin, double * half_cos


def twice(left, right):
    return (left[0] * right[0] - left[1] * right[1], left[1] * right[0] + left[0] * right[1])


def chain(start, step, count):
    terms = [start, twice(start, step)]
    double = step[0] + step[0]
    while len(terms) < count:
        (last_cos, last_sin), (cos, sin) = terms[-2:]
        terms.append((double * cos - last_cos, double * sin - last_sin))
    return terms


def flip(index, mask):
    bit = 1
    flipped = index
    while bit <= mask:
        if mask & bit:
            flipped = flipped + bit * (1 - 2 * lax.rem(lax.div(index, bit), 2))
        bit *= 2
    return flipped


def transform_kernel(
    device_count, strips_ref, tables_hbm, coords_ref, out_ref, gathered_ref,
    strip_ref, first_ref, mix_ref, second_ref, mixed_ref, turned_ref, everyone_ref, strip_sem, table_sem, own_sem,
    fs_send_sem, fs_recv_sem, core_send_sem, core_recv_sem
):
    me = lax.axis_index("fs")
    pol = lax.axis_index("pol")
    half = lax.rem(pol, 2)
    partner = {"pol": pol + 1 - 2 * half}
    facet_local = strip_ref.shape[0]
    slots = everyone_ref.shape[2] // 2
    span = min(SPAN, facet_local)
    pairs = span // 2

    order = []
    for group in range(facet_local // span):
        for pair in range(pairs):
            low = group * span + pairs - 1 - pair
            order.append((low, low + 2 * pair + 1))
    loads = [
        pltpu.make_async_copy(strips_ref.at[f], strip_ref.at[f], strip_sem.at[f])
        for f in range(facet_local)
    ]
    own = pltpu.make_async_copy(coords_ref, everyone_ref.at[me], own_sem)
    own.start()
    tables = [
        pltpu.make_async_copy(from_ref, to_ref, table_sem.at[i])
        for i, (from_ref, to_ref) in enumerate(
            [
                (tables_hbm.at[pl.ds(S + 1, 4)], mix_ref),
                (tables_hbm.at[pl.ds(0, S)], first_ref),
                (tables_hbm.at[S], second_ref),
            ]
        )
    ]
    tables[0].start()
    for i, (low, high) in enumerate(order):
        loads[low].start()
        loads[high].start()
        if i == 0:
            tables[1].start()
            tables[2].start()

    peers = [{"fs": flip(me, mask)} for mask in range(1, device_count)]
    barrier = pltpu.get_barrier_semaphore()
    for peer in [partner] + peers:
        pl.semaphore_signal(barrier, inc=1, device_id=peer, device_id_type=pl.DeviceIdType.MESH)

    def send(source, peer, send_sem, recv_sem, index):
        piece = everyone_ref.at[source, :, pl.ds(half * slots, slots)]
        copy = pltpu.make_async_remote_copy(
            src_ref=piece,
            dst_ref=piece,
            send_sem=send_sem.at[index],
            recv_sem=recv_sem.at[index],
            device_id=peer,
            device_id_type=pl.DeviceIdType.MESH,
        )
        copy.start()
        return copy

    sends = {}
    handed = []

    def hand_on(masks):
        for mask in masks:
            sends[mask].wait_recv()
            handed.append(send(flip(me, mask), partner, core_send_sem, core_recv_sem, mask - 1))

    tables[0].wait()
    mix = jnp.concatenate(
        [jnp.concatenate([mix_ref[2 * i], mix_ref[2 * i + 1]], axis=1) for i in range(2)], axis=0
    )

    def lanes(pieces):
        return jnp.concatenate(pieces, axis=1).astype(jnp.bfloat16)

    for group in range(facet_local // span):
        for pair in range(pairs):
            low, high = order[group * pairs + pair]
            loads[low].wait()
            loads[high].wait()

            def join(i, carry, low=low, high=high, pair=pair):
                rows = pl.ds(pl.multiple_of(i * CHUNK, CHUNK), CHUNK)
                both = jnp.dot(
                    jnp.concatenate([strip_ref[low, rows, :], strip_ref[high, rows, :]], axis=1),
                    mix,
                    preferred_element_type=jnp.float32,
                )
                for t in range(CHUNK // W):
                    to = pl.ds((i * (CHUNK // W) + t) * PITCH, W)
                    for part in range(2):
                        mixed_ref[2 * pair + part, to, :] = both[
                            W * t : W * (t + 1), LANES * part : LANES * (part + 1)
                        ]
                return carry

            lax.fori_loop(0, FH // CHUNK, join, 0)
            if group == 0 and pair == 0:
                pl.semaphore_wait(barrier, device_count)
                own.wait()
                for mask in reversed(range(1, device_count)):
                    sends[mask] = send(me, peers[mask - 1], fs_send_sem, fs_recv_sem, mask - 1)
        if group == 0:
            tables[1].wait()
            tables[2].wait()

        def put(to_ref, rows, product):
            for pair in range(pairs):
                for part in range(2):
                    to_ref[2 * pair + part, rows, :] = product[
                        W * part : W * (part + 1), LANES * pair : LANES * (pair + 1)
                    ]

        def take(from_ref, rows):
            return jnp.concatenate(
                [lanes([from_ref[2 * q + part, rows, :] for q in range(pairs)]) for part in range(2)],
                axis=0,
            )

        def first(i, carry):
            for u in range(UNROLL):
                rows = pl.ds(i * UNROLL + u, W, stride=PITCH)
                put(
                    turned_ref,
                    rows,
                    jnp.dot(
                        first_ref[i * UNROLL + u],
                        take(mixed_ref, rows),
                        preferred_element_type=jnp.float32,
                    ),
                )
            return carry

        lax.fori_loop(0, S // UNROLL, first, 0)

        def second(i, carry):
            for u in range(UNROLL):
                k = i * UNROLL + u
                put(
                    mixed_ref,
                    pl.ds(k, S, stride=PITCH),
                    jnp.dot(
                        second_ref[...],
                        take(turned_ref, pl.ds(k * PITCH, S)),
                        preferred_element_type=jnp.float32,
                    ),
                )
            return carry

        lax.fori_loop(0, W // UNROLL, second, 0)
        if group == facet_local // span - 1:
            hand_on(range(1, device_count // 2))

        def third(i, carry, group=group):
            for u in range(2):
                s = i * 2 + u
                out_ref[s, pl.ds(group * 2 * W, 2 * W), :] = take(mixed_ref, pl.ds(s * PITCH, W))
            return carry

        lax.fori_loop(0, S // 2, third, 0)

    hand_on(range(device_count // 2, device_count))
    for copy in handed:
        copy.wait_recv()
    for copy in list(sends.values()) + handed:
        copy.wait_send()
    gathered_ref[...] = everyone_ref[...]


def transform(strips, coords, device_count):
    vmem = pl.BlockSpec(memory_space=pltpu.VMEM)
    hbm = pl.BlockSpec(memory_space=pltpu.HBM)
    facet_local = strips.shape[0]
    span = min(SPAN, facet_local)
    scratch = pltpu.VMEM((span, S * PITCH, LANES), jnp.float32)
    kept = S * facet_local * 2 * W * W * 2 + device_count * coords.size * 4 + SLACK
    return pl.pallas_call(
        functools.partial(transform_kernel, device_count),
        out_shape=[
            jax.ShapeDtypeStruct((S, facet_local // span * 2 * W, span * W), jnp.bfloat16),
            jax.ShapeDtypeStruct((device_count,) + coords.shape, jnp.float32),
        ],
        in_specs=[hbm] * 3,
        out_specs=[vmem, vmem],
        scratch_shapes=[
            pltpu.VMEM((facet_local, FH, LANES), jnp.bfloat16),
            pltpu.VMEM((S, 2 * W, 2 * W), jnp.bfloat16),
            pltpu.VMEM((4, 2 * W, 2 * W), jnp.bfloat16),
            pltpu.VMEM((2 * S, 2 * S), jnp.bfloat16),
            scratch,
            scratch,
            pltpu.VMEM((device_count,) + coords.shape, jnp.float32),
            pltpu.SemaphoreType.DMA((facet_local,)),
            pltpu.SemaphoreType.DMA((3,)),
            pltpu.SemaphoreType.DMA,
            pltpu.SemaphoreType.DMA((device_count - 1,)),
            pltpu.SemaphoreType.DMA((device_count - 1,)),
            pltpu.SemaphoreType.DMA((device_count - 1,)),
            pltpu.SemaphoreType.DMA((device_count - 1,)),
        ],
        compiler_params=pltpu.CompilerParams(
            vmem_limit_bytes=VMEM_BYTES - kept, collective_id=0, has_side_effects=True
        ),
        cost_estimate=pl.CostEstimate(
            flops=5 * 10**9, bytes_accessed=16 * 2**20, transcendentals=0
        ),
    )(
        strips,
        pltpu.with_memory_space_constraint(jnp.asarray(transform_tables(), jnp.bfloat16), pltpu.HBM),
        pltpu.with_memory_space_constraint(coords, pltpu.HBM),
    )


def predict_kernel(
    facet_local, device_count, index_ref, owners_ref, counts_ref, coords_ref, windows_ref,
    limit_ref, kept_ref, sent_ref, out_ref, table_0_ref, table_1_ref, row_0_ref,
    row_1_ref, place_ref, load_ref, loads_ref
):
    lane = out_ref.shape[3]
    subgrids = owners_ref.shape[0]
    capacity = kept_ref.shape[0]
    span = min(SPAN, facet_local)
    groups = facet_local // span
    steps = span // 2
    first = index_ref[0] * facet_local
    unit = 1.0 / SG
    row_middle = (lax.div(first, R) * W).astype(jnp.float32) + (0.5 * (W - 1) - SG // 2)
    col_middle = (lax.rem(first, R) * W).astype(jnp.float32) + (0.5 * (span * W - 1) - SG // 2)
    ramp = lax.broadcasted_iota(jnp.int32, (8, lane), 0).astype(jnp.float32)
    fine = (ramp + 0.5) * unit
    second = ramp >= 4.0
    kind = jnp.where(second, ramp - 4.0, ramp)
    col_pick = jnp.where(kind == 1.0, 0.0, col_middle + (kind - 2.0) * (span * W))
    col_pick = jnp.where(kind == 0.0, 8.0, col_pick) * unit
    row_pick = jnp.where(kind == 0.0, 0.0, jnp.where(kind == 1.0, 8.0, row_middle)) * unit
    out_ref[...] = jnp.zeros_like(out_ref)

    def clear(ref):
        def body(i, carry):
            ref[i] = 0
            return carry

        lax.fori_loop(0, ref.shape[0], body, 0)

    clear(loads_ref)
    clear(limit_ref)
    me = index_ref[0]

    def rank(s, total):
        owner = owners_ref[s]
        load = loads_ref[owner]
        loads_ref[owner] = load + 1
        count = counts_ref[s]
        offset = owner ^ me
        load_ref[s] = load
        place_ref[s] = offset * capacity + load

        @pl.when(owner == me)
        def _():
            limit_ref[load] = count

        return total + lax.div(count + 1, 2)

    total = lax.fori_loop(0, subgrids, rank, 0)

    def following(s, b):
        items = []
        for _ in range(PAIRS):
            items.append((s, b))
            done = b + 2 >= counts_ref[s]
            end = jnp.logical_and(done, s == subgrids - 1)
            b = jnp.where(end, b, jnp.where(done, 0, b + 2))
            s = jnp.where(done, jnp.minimum(s + 1, subgrids - 1), s)
        return items, (s, b)

    def tables(u, refs, s, b):
        table_ref, row_ref = refs
        owner, load = owners_ref[s], load_ref[s]
        at = [[coords_ref[owner, axis, load, pl.ds(b + h, 1), :] for h in range(2)] for axis in range(2)]
        x, y = [jnp.where(second, one[1], one[0]) for one in at]
        picked = phase(x * row_pick + y * col_pick)
        row_ref[u, 2, :16] = jnp.concatenate(picked, axis=0)
        for h in range(2):
            col_step, row_step = [
                [jnp.broadcast_to(part[4 * h + i : 4 * h + i + 1], (8, lane)) for part in picked]
                for i in range(2)
            ]
            cols = chain(phase(at[1][h] * fine), col_step, steps * W // 8)
            entries = []
            for k in range(steps):
                some = cols[W // 8 * k : W // 8 * (k + 1)]
                entries += [cos for cos, _ in some] + [sin for _, sin in some]
            table_ref[u, h] = jnp.concatenate(entries, axis=0).astype(jnp.bfloat16)
            rows = chain(phase(at[0][h] * fine), row_step, W // 16)
            row_ref[u, h] = jnp.concatenate([cos for cos, _ in rows] + [sin for _, sin in rows], axis=0)

    def predict(u, refs, s, b):
        table_ref, row_ref = refs
        table = jnp.concatenate([table_ref[u, 0], table_ref[u, 1]], axis=1)
        grid = jnp.dot(windows_ref[s], table, preferred_element_type=jnp.float32)
        place = place_ref[s]
        for h in range(2):
            real = imag = None
            for g in range(groups):
                sums = []
                for part in range(2):
                    total = None
                    for k in range(W // 8):
                        at = (2 * g + part) * W + 8 * k
                        term = grid[at : at + 8, h * lane : (h + 1) * lane] * row_ref[
                            u, h, 8 * k : 8 * k + 8, :
                        ]
                        total = term if total is None else total + term
                    sums.append(total)
                at = 4 * h + 2 + g
                cos, sin = row_ref[u, 2, at : at + 1, :], row_ref[u, 2, 8 + at : 9 + at, :]
                more_real = sums[0] * cos + sums[1] * sin
                more_imag = sums[1] * cos - sums[0] * sin
                real = more_real if real is None else real + more_real
                imag = more_imag if imag is None else imag + more_imag
            out_ref[place, 0, pl.ds(b + h, 1), :] = jnp.sum(real, axis=0, keepdims=True)
            out_ref[place, 1, pl.ds(b + h, 1), :] = jnp.sum(imag, axis=0, keepdims=True)

    turns = [(table_0_ref, row_0_ref), (table_1_ref, row_1_ref)]
    items, after = following(0, 0)
    for u, (s, b) in enumerate(items):
        tables(u, turns[0], s, b)

    def step(i, carry):
        items, after = carry
        for turn in range(2):
            for u, (s, b) in enumerate(items):
                predict(u, turns[turn], s, b)
            items, after = following(*after)
            for u, (s, b) in enumerate(items):
                tables(u, turns[1 - turn], s, b)
        return items, after

    lax.fori_loop(0, lax.div(total + 2 * PAIRS - 1, 2 * PAIRS), step, (items, after))
    kept_ref[...] = out_ref[:capacity]
    sent_ref[...] = out_ref[capacity:].reshape(sent_ref.shape).astype(jnp.bfloat16)


def predict(windows, owners, counts, coords, device_index, facet_local):
    device_count, _, capacity, max_blocks, lane = coords.shape
    smem = pl.BlockSpec(memory_space=pltpu.SMEM)
    vmem = pl.BlockSpec(memory_space=pltpu.VMEM)
    slots = (capacity, 2, max_blocks, lane)
    return pl.pallas_call(
        functools.partial(predict_kernel, facet_local, device_count),
        out_shape=[
            jax.ShapeDtypeStruct((capacity,), jnp.int32),
            jax.ShapeDtypeStruct(slots, jnp.float32),
            jax.ShapeDtypeStruct((device_count - 1,) + slots, jnp.bfloat16),
        ],
        in_specs=[smem, smem, smem, vmem, vmem],
        out_specs=[smem, vmem, vmem],
        scratch_shapes=[
            pltpu.VMEM((device_count * capacity,) + slots[1:], jnp.float32),
            pltpu.VMEM((PAIRS, 2, windows.shape[2], lane), jnp.bfloat16),
            pltpu.VMEM((PAIRS, 2, windows.shape[2], lane), jnp.bfloat16),
            pltpu.VMEM((PAIRS, 3, W, lane), jnp.float32),
            pltpu.VMEM((PAIRS, 3, W, lane), jnp.float32),
            pltpu.SMEM((owners.shape[0],), jnp.int32),
            pltpu.SMEM((owners.shape[0],), jnp.int32),
            pltpu.SMEM((device_count,), jnp.int32),
        ],
        compiler_params=pltpu.CompilerParams(vmem_limit_bytes=16 * 2**20),
        cost_estimate=pl.CostEstimate(
            flops=2 * 10**10, bytes_accessed=2**20, transcendentals=0
        ),
    )(device_index.reshape(1), owners, counts, coords, windows)


def finish_kernel(
    parts, pols, limit_ref, stations_hbm, table_ref, kept_ref, parts_ref, out_ref, arrived_ref,
    station_ref, rows_ref, jones_ref, total_ref, sent_ref, station_sem, send_sem, recv_sem,
    pol_send_sem, pol_recv_sem
):
    me = lax.axis_index("fs")
    pol = lax.axis_index("pol")
    capacity, _, max_blocks, lane = total_ref.shape
    share = capacity // parts
    peers = [{"fs": flip(me, mask)} for mask in range(1, parts_ref.shape[0] + 1)]
    pol_peers = [{"pol": lax.rem(pol + step, pols)} for step in range(1, pols)]
    stations = pltpu.make_async_copy(stations_hbm, station_ref, station_sem)
    stations.start()
    barrier = pltpu.get_barrier_semaphore()
    for peer in peers + pol_peers:
        pl.semaphore_signal(
            barrier, inc=1, device_id=peer, device_id_type=pl.DeviceIdType.MESH
        )
    pl.semaphore_wait(barrier, len(peers) + len(pol_peers))
    copies = []
    for part in range(parts):
        slots = pl.ds(part * share, share)
        for i, peer in reversed(list(enumerate(peers))):
            copy = pltpu.make_async_remote_copy(
                src_ref=parts_ref.at[i, slots],
                dst_ref=arrived_ref.at[i, slots],
                send_sem=send_sem.at[part, i],
                recv_sem=recv_sem.at[part, i],
                device_id=peer,
                device_id_type=pl.DeviceIdType.MESH,
            )
            copy.start()
            copies.append(copy)
    stations.wait()
    chunks = table_ref.shape[1] // lane
    firsts = [4 * lax.div(pol, 2), 4 * lax.rem(pol, 2)]
    for row in range(table_ref.shape[0]):
        for chunk in range(chunks):
            at = row * chunks + chunk
            rows_ref[at : at + 1, :] = table_ref[row : row + 1, chunk * lane : (chunk + 1) * lane]

    def look_up(load, carry):
        for side in range(2):
            ids = station_ref[load, pl.ds(side, max_blocks, stride=2), :]
            low = ids & (lane - 1)
            high = ids >> (lane.bit_length() - 1)
            for row in range(4):
                entry = None
                for chunk in range(chunks):
                    source = jnp.broadcast_to(
                        rows_ref[pl.ds((firsts[side] + row) * chunks + chunk, 1), :],
                        (max_blocks, lane),
                    )
                    got = jnp.take_along_axis(source, low, axis=1, mode="promise_in_bounds")
                    entry = got if entry is None else jnp.where(high == chunk, got, entry)
                jones_ref[load, 4 * side + row] = entry
        return carry

    lax.fori_loop(0, capacity, look_up, 0)
    pol_copies = []
    for part in range(parts):
        slots = pl.ds(part * share, share)
        total = kept_ref[slots]
        for i in range(len(peers)):
            copies[part * len(peers) + len(peers) - 1 - i].wait_recv()
            total = total + arrived_ref[i, slots].astype(jnp.float32)
        total_ref[slots] = total
        sent_ref[pol, slots] = total.astype(jnp.bfloat16)
        for i, peer in enumerate(pol_peers):
            copy = pltpu.make_async_remote_copy(
                src_ref=sent_ref.at[pol, slots],
                dst_ref=sent_ref.at[pol, slots],
                send_sem=pol_send_sem.at[part, i],
                recv_sem=pol_recv_sem.at[part, i],
                device_id=peer,
                device_id_type=pl.DeviceIdType.MESH,
            )
            copy.start()
            pol_copies.append(copy)
    block = lax.broadcasted_iota(jnp.int32, (max_blocks, lane), 0)

    def product(a, b):
        return (a[0] * b[0] - a[1] * b[1], a[0] * b[1] + a[1] * b[0])

    def correct(load, carry):
        jones = [jones_ref[load, i] for i in range(8)]
        real = jnp.zeros((max_blocks, lane), jnp.float32)
        imag = jnp.zeros((max_blocks, lane), jnp.float32)
        for row in range(2):
            for col in range(2):
                comp = 2 * row + col
                visible = [
                    jnp.where(
                        pol == comp, total_ref[load, i], sent_ref[comp, load, i].astype(jnp.float32)
                    )
                    for i in range(2)
                ]
                step = product((jones[2 * row], jones[2 * row + 1]), visible)
                step = product(step, (jones[4 + 2 * col], -jones[5 + 2 * col]))
                real = real + step[0]
                imag = imag + step[1]
        keep = block < limit_ref[load]
        out_ref[0, load] = jnp.where(keep, real, 0.0)
        out_ref[1, load] = jnp.where(keep, imag, 0.0)
        return carry

    for part in range(parts):
        for copy in pol_copies[part * len(pol_peers) : (part + 1) * len(pol_peers)]:
            copy.wait_recv()
        lax.fori_loop(part * share, (part + 1) * share, correct, 0)
    for copy in copies + pol_copies:
        copy.wait_send()


def finish(limit, kept, sent, station_ids, table, pols):
    peers = sent.shape[0]
    slots = kept.shape
    capacity, _, max_blocks, lane = slots
    parts = max(1, min(capacity, 32 // (peers + 1)))
    smem = pl.BlockSpec(memory_space=pltpu.SMEM)
    vmem = pl.BlockSpec(memory_space=pltpu.VMEM)
    hbm = pl.BlockSpec(memory_space=pltpu.HBM)
    return pl.pallas_call(
        functools.partial(finish_kernel, parts, pols),
        out_shape=jax.ShapeDtypeStruct((2, capacity, max_blocks, lane), jnp.float32),
        in_specs=[smem, hbm, vmem, vmem, vmem],
        out_specs=vmem,
        scratch_shapes=[
            pltpu.VMEM((peers,) + slots, jnp.bfloat16),
            pltpu.VMEM((capacity, 2 * max_blocks, lane), jnp.int32),
            pltpu.VMEM((table.size // lane, lane), jnp.float32),
            pltpu.VMEM((capacity, 8, max_blocks, lane), jnp.float32),
            pltpu.VMEM(slots, jnp.float32),
            pltpu.VMEM((pols,) + slots, jnp.bfloat16),
            pltpu.SemaphoreType.DMA,
            pltpu.SemaphoreType.DMA((parts, peers)),
            pltpu.SemaphoreType.DMA((parts, peers)),
            pltpu.SemaphoreType.DMA((parts, pols - 1)),
            pltpu.SemaphoreType.DMA((parts, pols - 1)),
        ],
        compiler_params=pltpu.CompilerParams(
            vmem_limit_bytes=8 * 2**20, collective_id=1, has_side_effects=True
        ),
    )(
        limit,
        pltpu.with_memory_space_constraint(
            station_ids.reshape(capacity, 2 * max_blocks, lane), pltpu.HBM
        ),
        table,
        kept,
        sent,
    )


def on_device(facets, owners, counts, coords, station_ids, jones_table):
    device_index = lax.axis_index("fs").astype(jnp.int32)
    device_count, pols = lax.axis_size("fs"), lax.axis_size("pol")
    windows, all_coords = transform(facets[0], coords, device_count)
    limit, kept, sent = predict(
        windows, owners, counts, all_coords, device_index, facets.shape[1]
    )
    return finish(limit, kept, sent, station_ids, jones_table, pols)[None]


def solution(mesh):
    return jax.shard_map(
        on_device,
        mesh=mesh,
        in_specs=(
            P("pol", "fs", None, None),
            P(),
            P(),
            P(None, "fs", None, None),
            P("fs", None, None, None),
            P(),
        ),
        out_specs=P("pol", None, "fs", None, None),
        check_vma=False,
    )
```

```python
import functools
import math

import jax
import jax.numpy as jnp
import numpy as np
from jax import lax
from jax.experimental import pallas as pl
from jax.experimental.pallas import tpu as pltpu
from jax.sharding import PartitionSpec as P

R = 8
W = 64
S = 64
FH = 4096
SG = 512
LANES = 128
SPAN = 4
PITCH = 65
CHUNK = 2048
UNROLL = 64
PAIRS = 3
SHARES = 2
VMEM_BYTES = 67043328
SLACK = 13000 * 1024


def fit(values, terms):
    series = np.polynomial.chebyshev.Chebyshev.interpolate(
        lambda square: values(np.sqrt(np.maximum(square, 1e-12))), terms - 1, domain=[0.0, 0.25]
    )
    return [float(c) for c in series.convert(kind=np.polynomial.Polynomial).coef]


SIN_COEFS = fit(lambda r: np.sin(np.pi * r) / r, 5)
COS_COEFS = fit(lambda r: np.cos(np.pi * r), 5)


def unit_circle(turns):
    return np.exp(-2j * np.pi * turns)


def as_real(table):
    return np.concatenate(
        [
            np.concatenate([table.real, -table.imag], axis=-1),
            np.concatenate([table.imag, table.real], axis=-1),
        ],
        axis=-2,
    )


def mix_table():
    table = np.zeros((4 * W, 4 * W))
    col = np.arange(W)
    mirror = W - 1 - col
    a_real, a_imag, b_real, b_imag = mirror, W + mirror, 2 * W + col, 3 * W + col
    table[b_real, col] = table[a_real, col] = 1.0
    table[b_imag, W + col] = 1.0
    table[a_imag, W + col] = -1.0
    table[b_imag, 2 * W + col] = table[a_imag, 2 * W + col] = 1.0
    table[b_real, 3 * W + col] = -1.0
    table[a_real, 3 * W + col] = 1.0
    return table


def first_tables():
    n1 = np.arange(S)[:, None, None]
    k1 = np.arange(W)[None, :, None]
    n2 = np.arange(W)[None, None, :]
    rows = unit_circle((k1 * n2 % W) / W + (n1 * k1 % FH) / FH)
    upper, lower = rows[:, W // 2 :], rows[:, W // 2 - 1 :: -1]
    return as_real(np.concatenate([upper + lower, -1j * (upper - lower)], axis=1))


def second_table():
    index = np.arange(S)
    table = unit_circle((index[:, None] * index[None, :] % S) / S)
    return as_real(table) / (math.sqrt(FH) * SG)


def transform_tables():
    mix = mix_table().reshape(2, 2 * W, 2, 2 * W).transpose(0, 2, 1, 3).reshape(4, 2 * W, 2 * W)
    return np.concatenate([first_tables(), second_table()[None], mix])


def horner(coefs, square):
    total = jnp.full_like(square, coefs[-1])
    for coef in coefs[-2::-1]:
        total = total * square + coef
    return total


def phase(turns):
    rest = turns - jnp.round(turns)
    square = rest * rest
    half_cos = horner(COS_COEFS, square)
    half_sin = horner(SIN_COEFS, square) * rest
    double = half_sin + half_sin
    return 1.0 - double * half_sin, double * half_cos


def twice(left, right):
    return (left[0] * right[0] - left[1] * right[1], left[1] * right[0] + left[0] * right[1])


def chain(start, step, count):
    terms = [start, twice(start, step)]
    double = step[0] + step[0]
    while len(terms) < count:
        (last_cos, last_sin), (cos, sin) = terms[-2:]
        terms.append((double * cos - last_cos, double * sin - last_sin))
    return terms


def flip(index, mask):
    bit = 1
    flipped = index
    while bit <= mask:
        if mask & bit:
            flipped = flipped + bit * (1 - 2 * lax.rem(lax.div(index, bit), 2))
        bit *= 2
    return flipped


def transform_kernel(
    device_count, strips_ref, tables_hbm, coords_ref, out_ref, gathered_ref,
    strip_ref, first_ref, mix_ref, second_ref, mixed_ref, turned_ref, everyone_ref, strip_sem, table_sem, own_sem,
    pair_send_sem, pair_recv_sem, line_send_sem, line_recv_sem, core_send_sem, core_recv_sem
):
    me = lax.axis_index("fs")
    pol = lax.axis_index("pol")
    half = lax.rem(pol, 2)
    partner = {"pol": pol + 1 - 2 * half}
    facet_local = strip_ref.shape[0]
    slots = everyone_ref.shape[2] // 2
    span = min(SPAN, facet_local)
    pairs = span // 2

    order = []
    for group in range(facet_local // span):
        for pair in range(pairs):
            low = group * span + pairs - 1 - pair
            order.append((low, low + 2 * pair + 1))
    loads = [
        pltpu.make_async_copy(strips_ref.at[f], strip_ref.at[f], strip_sem.at[f])
        for f in range(facet_local)
    ]
    own = pltpu.make_async_copy(coords_ref, everyone_ref.at[me], own_sem)
    own.start()
    tables = [
        pltpu.make_async_copy(from_ref, to_ref, table_sem.at[i])
        for i, (from_ref, to_ref) in enumerate(
            [
                (tables_hbm.at[pl.ds(S + 1, 4)], mix_ref),
                (tables_hbm.at[pl.ds(0, S)], first_ref),
                (tables_hbm.at[S], second_ref),
            ]
        )
    ]
    tables[0].start()
    for i, (low, high) in enumerate(order):
        loads[low].start()
        loads[high].start()
        if i == 0:
            tables[1].start()
            tables[2].start()

    across = {"fs": flip(me, 1)}
    line = {h: {"fs": flip(me, 2 * h)} for h in range(1, device_count // 2)}
    barrier = pltpu.get_barrier_semaphore()
    for peer in [partner, across] + list(line.values()):
        pl.semaphore_signal(barrier, inc=1, device_id=peer, device_id_type=pl.DeviceIdType.MESH)

    def send(source, peer, send_sem, recv_sem, index):
        piece = everyone_ref.at[source, :, pl.ds(half * slots, slots)]
        copy = pltpu.make_async_remote_copy(
            src_ref=piece,
            dst_ref=piece,
            send_sem=send_sem.at[index],
            recv_sem=recv_sem.at[index],
            device_id=peer,
            device_id_type=pl.DeviceIdType.MESH,
        )
        copy.start()
        return copy

    along = {}
    crossed = {}
    handed = []

    def to_partner(mask):
        handed.append(send(flip(me, mask), partner, core_send_sem, core_recv_sem, mask - 1))

    def relay():
        crossed[0].wait_recv()
        to_partner(1)
        for h in line:
            along[h].wait_recv()
            crossed[h] = send(flip(me, 2 * h), across, pair_send_sem, pair_recv_sem, h)
            to_partner(2 * h)

    def hand_on():
        for h in line:
            crossed[h].wait_recv()
            to_partner(2 * h + 1)

    tables[0].wait()
    mix = jnp.concatenate(
        [jnp.concatenate([mix_ref[2 * i], mix_ref[2 * i + 1]], axis=1) for i in range(2)], axis=0
    )

    def lanes(pieces):
        return jnp.concatenate(pieces, axis=1).astype(jnp.bfloat16)

    for group in range(facet_local // span):
        for pair in range(pairs):
            low, high = order[group * pairs + pair]
            loads[low].wait()
            loads[high].wait()

            def join(i, carry, low=low, high=high, pair=pair):
                rows = pl.ds(pl.multiple_of(i * CHUNK, CHUNK), CHUNK)
                both = jnp.dot(
                    jnp.concatenate([strip_ref[low, rows, :], strip_ref[high, rows, :]], axis=1),
                    mix,
                    preferred_element_type=jnp.float32,
                )
                for t in range(CHUNK // W):
                    to = pl.ds((i * (CHUNK // W) + t) * PITCH, W)
                    for part in range(2):
                        mixed_ref[2 * pair + part, to, :] = both[
                            W * t : W * (t + 1), LANES * part : LANES * (part + 1)
                        ]
                return carry

            lax.fori_loop(0, FH // CHUNK, join, 0)
            if group == 0 and pair == 0:
                pl.semaphore_wait(barrier, device_count // 2 + 1)
                own.wait()
                for h in reversed(list(line)):
                    along[h] = send(me, line[h], line_send_sem, line_recv_sem, h - 1)
                crossed[0] = send(me, across, pair_send_sem, pair_recv_sem, 0)
        if group == 0:
            tables[1].wait()
            tables[2].wait()

        def put(to_ref, rows, product):
            for pair in range(pairs):
                for part in range(2):
                    to_ref[2 * pair + part, rows, :] = product[
                        W * part : W * (part + 1), LANES * pair : LANES * (pair + 1)
                    ]

        def take(from_ref, rows):
            return jnp.concatenate(
                [lanes([from_ref[2 * q + part, rows, :] for q in range(pairs)]) for part in range(2)],
                axis=0,
            )

        def first(i, carry):
            for u in range(UNROLL):
                rows = pl.ds(i * UNROLL + u, W, stride=PITCH)
                put(
                    turned_ref,
                    rows,
                    jnp.dot(
                        first_ref[i * UNROLL + u],
                        take(mixed_ref, rows),
                        preferred_element_type=jnp.float32,
                    ),
                )
            return carry

        lax.fori_loop(0, S // UNROLL, first, 0)

        def second(i, carry):
            for u in range(UNROLL):
                k = i * UNROLL + u
                put(
                    mixed_ref,
                    pl.ds(k, S, stride=PITCH),
                    jnp.dot(
                        second_ref[...],
                        take(turned_ref, pl.ds(k * PITCH, S)),
                        preferred_element_type=jnp.float32,
                    ),
                )
            return carry

        lax.fori_loop(0, W // UNROLL, second, 0)
        if group == 0:
            relay()
        if group == facet_local // span - 1:
            hand_on()

        def third(i, carry, group=group):
            for u in range(2):
                s = i * 2 + u
                out_ref[s, pl.ds(group * 2 * W, 2 * W), :] = take(mixed_ref, pl.ds(s * PITCH, W))
            return carry

        lax.fori_loop(0, S // 2, third, 0)

    for copy in handed:
        copy.wait_recv()
    for copy in list(along.values()) + list(crossed.values()) + handed:
        copy.wait_send()
    gathered_ref[...] = everyone_ref[...]


def transform(strips, coords, device_count):
    vmem = pl.BlockSpec(memory_space=pltpu.VMEM)
    hbm = pl.BlockSpec(memory_space=pltpu.HBM)
    facet_local = strips.shape[0]
    span = min(SPAN, facet_local)
    scratch = pltpu.VMEM((span, S * PITCH, LANES), jnp.float32)
    kept = S * facet_local * 2 * W * W * 2 + device_count * coords.size * 4 + SLACK
    return pl.pallas_call(
        functools.partial(transform_kernel, device_count),
        out_shape=[
            jax.ShapeDtypeStruct((S, facet_local // span * 2 * W, span * W), jnp.bfloat16),
            jax.ShapeDtypeStruct((device_count,) + coords.shape, jnp.float32),
        ],
        in_specs=[hbm] * 3,
        out_specs=[vmem, vmem],
        scratch_shapes=[
            pltpu.VMEM((facet_local, FH, LANES), jnp.bfloat16),
            pltpu.VMEM((S, 2 * W, 2 * W), jnp.bfloat16),
            pltpu.VMEM((4, 2 * W, 2 * W), jnp.bfloat16),
            pltpu.VMEM((2 * S, 2 * S), jnp.bfloat16),
            scratch,
            scratch,
            pltpu.VMEM((device_count,) + coords.shape, jnp.float32),
            pltpu.SemaphoreType.DMA((facet_local,)),
            pltpu.SemaphoreType.DMA((3,)),
            pltpu.SemaphoreType.DMA,
            pltpu.SemaphoreType.DMA((device_count // 2,)),
            pltpu.SemaphoreType.DMA((device_count // 2,)),
            pltpu.SemaphoreType.DMA((device_count // 2 - 1,)),
            pltpu.SemaphoreType.DMA((device_count // 2 - 1,)),
            pltpu.SemaphoreType.DMA((device_count - 1,)),
            pltpu.SemaphoreType.DMA((device_count - 1,)),
        ],
        compiler_params=pltpu.CompilerParams(
            vmem_limit_bytes=VMEM_BYTES - kept, collective_id=0, has_side_effects=True
        ),
        cost_estimate=pl.CostEstimate(
            flops=5 * 10**9, bytes_accessed=16 * 2**20, transcendentals=0
        ),
    )(
        strips,
        pltpu.with_memory_space_constraint(jnp.asarray(transform_tables(), jnp.bfloat16), pltpu.HBM),
        pltpu.with_memory_space_constraint(coords, pltpu.HBM),
    )


def predict_kernel(
    facet_local, device_count, index_ref, owners_ref, counts_ref, coords_ref, windows_ref,
    limit_ref, kept_ref, sent_ref, out_ref, table_0_ref, table_1_ref, row_0_ref,
    row_1_ref, place_ref, load_ref, loads_ref
):
    lane = out_ref.shape[3]
    subgrids = owners_ref.shape[0]
    half, capacity = kept_ref.shape[:2]
    span = min(SPAN, facet_local)
    groups = facet_local // span
    steps = span // 2
    first = index_ref[0] * facet_local
    unit = 1.0 / SG
    row_middle = (lax.div(first, R) * W).astype(jnp.float32) + (0.5 * (W - 1) - SG // 2)
    col_middle = (lax.rem(first, R) * W).astype(jnp.float32) + (0.5 * (span * W - 1) - SG // 2)
    ramp = lax.broadcasted_iota(jnp.int32, (8, lane), 0).astype(jnp.float32)
    fine = (ramp + 0.5) * unit
    second = ramp >= 4.0
    kind = jnp.where(second, ramp - 4.0, ramp)
    col_pick = jnp.where(kind == 1.0, 0.0, col_middle + (kind - 2.0) * (span * W))
    col_pick = jnp.where(kind == 0.0, 8.0, col_pick) * unit
    row_pick = jnp.where(kind == 0.0, 0.0, jnp.where(kind == 1.0, 8.0, row_middle)) * unit
    out_ref[...] = jnp.zeros_like(out_ref)

    def clear(ref):
        def body(i, carry):
            ref[i] = 0
            return carry

        lax.fori_loop(0, ref.shape[0], body, 0)

    clear(loads_ref)
    clear(limit_ref)
    me = index_ref[0]

    def rank(s, total):
        owner = owners_ref[s]
        load = loads_ref[owner]
        loads_ref[owner] = load + 1
        count = counts_ref[s]
        offset = owner ^ me
        load_ref[s] = load
        place_ref[s] = ((offset & 1) * half + (offset >> 1)) * capacity + load

        @pl.when(owner == me)
        def _():
            limit_ref[load] = count

        return total + lax.div(count + 1, 2)

    total = lax.fori_loop(0, subgrids, rank, 0)

    def following(s, b):
        items = []
        for _ in range(PAIRS):
            items.append((s, b))
            done = b + 2 >= counts_ref[s]
            end = jnp.logical_and(done, s == subgrids - 1)
            b = jnp.where(end, b, jnp.where(done, 0, b + 2))
            s = jnp.where(done, jnp.minimum(s + 1, subgrids - 1), s)
        return items, (s, b)

    def tables(u, refs, s, b):
        table_ref, row_ref = refs
        owner, load = owners_ref[s], load_ref[s]
        at = [[coords_ref[owner, axis, load, pl.ds(b + h, 1), :] for h in range(2)] for axis in range(2)]
        x, y = [jnp.where(second, one[1], one[0]) for one in at]
        picked = phase(x * row_pick + y * col_pick)
        row_ref[u, 2, :16] = jnp.concatenate(picked, axis=0)
        for h in range(2):
            col_step, row_step = [
                [jnp.broadcast_to(part[4 * h + i : 4 * h + i + 1], (8, lane)) for part in picked]
                for i in range(2)
            ]
            cols = chain(phase(at[1][h] * fine), col_step, steps * W // 8)
            entries = []
            for k in range(steps):
                some = cols[W // 8 * k : W // 8 * (k + 1)]
                entries += [cos for cos, _ in some] + [sin for _, sin in some]
            table_ref[u, h] = jnp.concatenate(entries, axis=0).astype(jnp.bfloat16)
            rows = chain(phase(at[0][h] * fine), row_step, W // 16)
            row_ref[u, h] = jnp.concatenate([cos for cos, _ in rows] + [sin for _, sin in rows], axis=0)

    def predict(u, refs, s, b):
        table_ref, row_ref = refs
        table = jnp.concatenate([table_ref[u, 0], table_ref[u, 1]], axis=1)
        grid = jnp.dot(windows_ref[s], table, preferred_element_type=jnp.float32)
        place = place_ref[s]
        for h in range(2):
            real = imag = None
            for g in range(groups):
                sums = []
                for part in range(2):
                    total = None
                    for k in range(W // 8):
                        at = (2 * g + part) * W + 8 * k
                        term = grid[at : at + 8, h * lane : (h + 1) * lane] * row_ref[
                            u, h, 8 * k : 8 * k + 8, :
                        ]
                        total = term if total is None else total + term
                    sums.append(total)
                at = 4 * h + 2 + g
                cos, sin = row_ref[u, 2, at : at + 1, :], row_ref[u, 2, 8 + at : 9 + at, :]
                more_real = sums[0] * cos + sums[1] * sin
                more_imag = sums[1] * cos - sums[0] * sin
                real = more_real if real is None else real + more_real
                imag = more_imag if imag is None else imag + more_imag
            out_ref[place, 0, pl.ds(b + h, 1), :] = jnp.sum(real, axis=0, keepdims=True)
            out_ref[place, 1, pl.ds(b + h, 1), :] = jnp.sum(imag, axis=0, keepdims=True)

    turns = [(table_0_ref, row_0_ref), (table_1_ref, row_1_ref)]
    items, after = following(0, 0)
    for u, (s, b) in enumerate(items):
        tables(u, turns[0], s, b)

    def step(i, carry):
        items, after = carry
        for turn in range(2):
            for u, (s, b) in enumerate(items):
                predict(u, turns[turn], s, b)
            items, after = following(*after)
            for u, (s, b) in enumerate(items):
                tables(u, turns[1 - turn], s, b)
        return items, after

    lax.fori_loop(0, lax.div(total + 2 * PAIRS - 1, 2 * PAIRS), step, (items, after))
    kept_ref[...] = out_ref[: half * capacity].reshape(kept_ref.shape)
    sent_ref[...] = out_ref[half * capacity :].reshape(sent_ref.shape).astype(jnp.bfloat16)


def predict(windows, owners, counts, coords, device_index, facet_local):
    device_count, _, capacity, max_blocks, lane = coords.shape
    smem = pl.BlockSpec(memory_space=pltpu.SMEM)
    vmem = pl.BlockSpec(memory_space=pltpu.VMEM)
    slots = (capacity, 2, max_blocks, lane)
    return pl.pallas_call(
        functools.partial(predict_kernel, facet_local, device_count),
        out_shape=[
            jax.ShapeDtypeStruct((capacity,), jnp.int32),
            jax.ShapeDtypeStruct((device_count // 2,) + slots, jnp.float32),
            jax.ShapeDtypeStruct((device_count // 2,) + slots, jnp.bfloat16),
        ],
        in_specs=[smem, smem, smem, vmem, vmem],
        out_specs=[smem, vmem, vmem],
        scratch_shapes=[
            pltpu.VMEM((device_count * capacity,) + slots[1:], jnp.float32),
            pltpu.VMEM((PAIRS, 2, windows.shape[2], lane), jnp.bfloat16),
            pltpu.VMEM((PAIRS, 2, windows.shape[2], lane), jnp.bfloat16),
            pltpu.VMEM((PAIRS, 3, W, lane), jnp.float32),
            pltpu.VMEM((PAIRS, 3, W, lane), jnp.float32),
            pltpu.SMEM((owners.shape[0],), jnp.int32),
            pltpu.SMEM((owners.shape[0],), jnp.int32),
            pltpu.SMEM((device_count,), jnp.int32),
        ],
        compiler_params=pltpu.CompilerParams(
            vmem_limit_bytes=16 * 2**20
        ),
        cost_estimate=pl.CostEstimate(
            flops=2 * 10**10, bytes_accessed=2**20, transcendentals=0
        ),
    )(device_index.reshape(1), owners, counts, coords, windows)


def finish_kernel(
    parts, pols, limit_ref, stations_hbm, table_ref, kept_ref, cross_ref, out_ref, pair_ref, line_ref,
    partial_ref, station_ref, rows_ref, jones_ref, total_ref, sent_ref, station_sem, pair_send_sem,
    pair_recv_sem, line_send_sem, line_recv_sem, pol_send_sem, pol_recv_sem
):
    me = lax.axis_index("fs")
    pol = lax.axis_index("pol")
    half = kept_ref.shape[0]
    capacity, _, max_blocks, lane = total_ref.shape
    share = capacity // parts
    shares = [pl.ds(part * share, share) for part in range(parts)]
    across = {"fs": flip(me, 1)}
    line = [{"fs": flip(me, 2 * h)} for h in range(1, half)]
    pol_peers = [{"pol": lax.rem(pol + step, pols)} for step in range(1, pols)]
    stations = pltpu.make_async_copy(stations_hbm, station_ref, station_sem)
    stations.start()
    barrier = pltpu.get_barrier_semaphore()
    for peer in [across] + line + pol_peers:
        pl.semaphore_signal(
            barrier, inc=1, device_id=peer, device_id_type=pl.DeviceIdType.MESH
        )
    pl.semaphore_wait(barrier, half + pols - 1)

    def send(from_ref, to_ref, send_sem, recv_sem, peer):
        copy = pltpu.make_async_remote_copy(
            src_ref=from_ref,
            dst_ref=to_ref,
            send_sem=send_sem,
            recv_sem=recv_sem,
            device_id=peer,
            device_id_type=pl.DeviceIdType.MESH,
        )
        copy.start()
        return copy

    order = [(part, h) for part in range(parts) for h in reversed(range(half))]
    crossing = {
        (part, h): send(
            cross_ref.at[h, shares[part]],
            pair_ref.at[h, shares[part]],
            pair_send_sem.at[part, h],
            pair_recv_sem.at[part, h],
            across,
        )
        for part, h in order
    }
    stations.wait()
    chunks = table_ref.shape[1] // lane
    firsts = [4 * lax.div(pol, 2), 4 * lax.rem(pol, 2)]
    for row in range(table_ref.shape[0]):
        for chunk in range(chunks):
            at = row * chunks + chunk
            rows_ref[at : at + 1, :] = table_ref[row : row + 1, chunk * lane : (chunk + 1) * lane]

    def look_up(load, carry):
        for side in range(2):
            ids = station_ref[load, pl.ds(side, max_blocks, stride=2), :]
            low = ids & (lane - 1)
            high = ids >> (lane.bit_length() - 1)
            for row in range(4):
                entry = None
                for chunk in range(chunks):
                    source = jnp.broadcast_to(
                        rows_ref[pl.ds((firsts[side] + row) * chunks + chunk, 1), :],
                        (max_blocks, lane),
                    )
                    got = jnp.take_along_axis(source, low, axis=1, mode="promise_in_bounds")
                    entry = got if entry is None else jnp.where(high == chunk, got, entry)
                jones_ref[load, 4 * side + row] = entry
        return carry

    lax.fori_loop(0, capacity, look_up, 0)
    along = {}
    for part, h in order:
        slots = shares[part]
        crossing[part, h].wait_recv()
        joined = kept_ref[h, slots] + pair_ref[h, slots].astype(jnp.float32)
        if h == 0:
            total_ref[slots] = joined
            continue
        partial_ref[h - 1, slots] = joined.astype(jnp.bfloat16)
        along[part, h] = send(
            partial_ref.at[h - 1, slots],
            line_ref.at[h - 1, slots],
            line_send_sem.at[part, h - 1],
            line_recv_sem.at[part, h - 1],
            line[h - 1],
        )
    exchanged = {}
    for part, slots in enumerate(shares):
        total = total_ref[slots]
        for h in range(1, half):
            along[part, h].wait_recv()
            total = total + line_ref[h - 1, slots].astype(jnp.float32)
        total_ref[slots] = total
        sent_ref[pol, slots] = total.astype(jnp.bfloat16)
        for i, peer in enumerate(pol_peers):
            mine = sent_ref.at[pol, slots]
            exchanged[part, i] = send(
                mine, mine, pol_send_sem.at[part, i], pol_recv_sem.at[part, i], peer
            )
    block = lax.broadcasted_iota(jnp.int32, (max_blocks, lane), 0)

    def product(a, b):
        return (a[0] * b[0] - a[1] * b[1], a[0] * b[1] + a[1] * b[0])

    def correct(load, carry):
        jones = [jones_ref[load, i] for i in range(8)]
        real = jnp.zeros((max_blocks, lane), jnp.float32)
        imag = jnp.zeros((max_blocks, lane), jnp.float32)
        for row in range(2):
            for col in range(2):
                comp = 2 * row + col
                visible = [
                    jnp.where(
                        pol == comp, total_ref[load, i], sent_ref[comp, load, i].astype(jnp.float32)
                    )
                    for i in range(2)
                ]
                step = product((jones[2 * row], jones[2 * row + 1]), visible)
                step = product(step, (jones[4 + 2 * col], -jones[5 + 2 * col]))
                real = real + step[0]
                imag = imag + step[1]
        keep = block < limit_ref[load]
        out_ref[0, load] = jnp.where(keep, real, 0.0)
        out_ref[1, load] = jnp.where(keep, imag, 0.0)
        return carry

    for part in range(parts):
        for i in range(len(pol_peers)):
            exchanged[part, i].wait_recv()
        lax.fori_loop(part * share, (part + 1) * share, correct, 0)
    for copies in (crossing, along, exchanged):
        for copy in copies.values():
            copy.wait_send()


def finish(limit, kept, sent, station_ids, table, pols):
    half = kept.shape[0]
    slots = kept.shape[1:]
    capacity, _, max_blocks, lane = slots
    parts = max(1, min(SHARES, 16 // half))
    smem = pl.BlockSpec(memory_space=pltpu.SMEM)
    vmem = pl.BlockSpec(memory_space=pltpu.VMEM)
    hbm = pl.BlockSpec(memory_space=pltpu.HBM)
    return pl.pallas_call(
        functools.partial(finish_kernel, parts, pols),
        out_shape=jax.ShapeDtypeStruct((2, capacity, max_blocks, lane), jnp.float32),
        in_specs=[smem, hbm, vmem, vmem, vmem],
        out_specs=vmem,
        scratch_shapes=[
            pltpu.VMEM((half,) + slots, jnp.bfloat16),
            pltpu.VMEM((half - 1,) + slots, jnp.bfloat16),
            pltpu.VMEM((half - 1,) + slots, jnp.bfloat16),
            pltpu.VMEM((capacity, 2 * max_blocks, lane), jnp.int32),
            pltpu.VMEM((table.size // lane, lane), jnp.float32),
            pltpu.VMEM((capacity, 8, max_blocks, lane), jnp.float32),
            pltpu.VMEM(slots, jnp.float32),
            pltpu.VMEM((pols,) + slots, jnp.bfloat16),
            pltpu.SemaphoreType.DMA,
            pltpu.SemaphoreType.DMA((parts, half)),
            pltpu.SemaphoreType.DMA((parts, half)),
            pltpu.SemaphoreType.DMA((parts, half - 1)),
            pltpu.SemaphoreType.DMA((parts, half - 1)),
            pltpu.SemaphoreType.DMA((parts, pols - 1)),
            pltpu.SemaphoreType.DMA((parts, pols - 1)),
        ],
        compiler_params=pltpu.CompilerParams(
            vmem_limit_bytes=8 * 2**20, collective_id=1, has_side_effects=True
        ),
    )(
        limit,
        pltpu.with_memory_space_constraint(
            station_ids.reshape(capacity, 2 * max_blocks, lane), pltpu.HBM
        ),
        table,
        kept,
        sent,
    )


def on_device(facets, owners, counts, coords, station_ids, jones_table):
    device_index = lax.axis_index("fs").astype(jnp.int32)
    device_count, pols = lax.axis_size("fs"), lax.axis_size("pol")
    windows, all_coords = transform(facets[0], coords, device_count)
    limit, kept, sent = predict(
        windows, owners, counts, all_coords, device_index, facets.shape[1]
    )
    return finish(limit, kept, sent, station_ids, jones_table, pols)[None]


def solution(mesh):
    return jax.shard_map(
        on_device,
        mesh=mesh,
        in_specs=(
            P("pol", "fs", None, None),
            P(),
            P(),
            P(None, "fs", None, None),
            P("fs", None, None, None),
            P(),
        ),
        out_specs=P("pol", None, "fs", None, None),
        check_vma=False,
    )
```

```python
import functools
import math

import jax
import jax.numpy as jnp
import numpy as np
from jax import lax
from jax.experimental import pallas as pl
from jax.experimental.pallas import tpu as pltpu
from jax.sharding import PartitionSpec as P

R = 8
W = 64
S = 64
FH = 4096
SG = 512
LANES = 128
SPAN = 4
PITCH = 65
CHUNK = 2048
UNROLL = 64
PAIRS = 3
SHARES = 2
VMEM_BYTES = 67043328
SLACK = 13000 * 1024


def fit(values, terms):
    series = np.polynomial.chebyshev.Chebyshev.interpolate(
        lambda square: values(np.sqrt(np.maximum(square, 1e-12))), terms - 1, domain=[0.0, 0.25]
    )
    return [float(c) for c in series.convert(kind=np.polynomial.Polynomial).coef]


SIN_COEFS = fit(lambda r: np.sin(np.pi * r) / r, 5)
COS_COEFS = fit(lambda r: np.cos(np.pi * r), 5)


def unit_circle(turns):
    return np.exp(-2j * np.pi * turns)


def as_real(table):
    return np.concatenate(
        [
            np.concatenate([table.real, -table.imag], axis=-1),
            np.concatenate([table.imag, table.real], axis=-1),
        ],
        axis=-2,
    )


def mix_table():
    table = np.zeros((4 * W, 4 * W))
    col = np.arange(W)
    mirror = W - 1 - col
    a_real, a_imag, b_real, b_imag = mirror, W + mirror, 2 * W + col, 3 * W + col
    table[b_real, col] = table[a_real, col] = 1.0
    table[b_imag, W + col] = 1.0
    table[a_imag, W + col] = -1.0
    table[b_imag, 2 * W + col] = table[a_imag, 2 * W + col] = 1.0
    table[b_real, 3 * W + col] = -1.0
    table[a_real, 3 * W + col] = 1.0
    return table


def first_tables():
    n1 = np.arange(S)[:, None, None]
    k1 = np.arange(W)[None, :, None]
    n2 = np.arange(W)[None, None, :]
    rows = unit_circle((k1 * n2 % W) / W + (n1 * k1 % FH) / FH)
    upper, lower = rows[:, W // 2 :], rows[:, W // 2 - 1 :: -1]
    return as_real(np.concatenate([upper + lower, -1j * (upper - lower)], axis=1))


def second_table():
    index = np.arange(S)
    table = unit_circle((index[:, None] * index[None, :] % S) / S)
    return as_real(table) / (math.sqrt(FH) * SG)


def transform_tables():
    mix = mix_table().reshape(2, 2 * W, 2, 2 * W).transpose(0, 2, 1, 3).reshape(4, 2 * W, 2 * W)
    return np.concatenate([first_tables(), second_table()[None], mix])


def horner(coefs, square):
    total = jnp.full_like(square, coefs[-1])
    for coef in coefs[-2::-1]:
        total = total * square + coef
    return total


def phase(turns):
    rest = turns - jnp.round(turns)
    square = rest * rest
    half_cos = horner(COS_COEFS, square)
    half_sin = horner(SIN_COEFS, square) * rest
    double = half_sin + half_sin
    return 1.0 - double * half_sin, double * half_cos


def twice(left, right):
    return (left[0] * right[0] - left[1] * right[1], left[1] * right[0] + left[0] * right[1])


def chain(start, step, count):
    terms = [start, twice(start, step)]
    double = step[0] + step[0]
    while len(terms) < count:
        (last_cos, last_sin), (cos, sin) = terms[-2:]
        terms.append((double * cos - last_cos, double * sin - last_sin))
    return terms


def flip(index, mask):
    bit = 1
    flipped = index
    while bit <= mask:
        if mask & bit:
            flipped = flipped + bit * (1 - 2 * lax.rem(lax.div(index, bit), 2))
        bit *= 2
    return flipped


def transform_kernel(
    device_count, strips_ref, tables_hbm, coords_ref, out_ref, gathered_ref,
    strip_ref, first_ref, mix_ref, second_ref, mixed_ref, turned_ref, everyone_ref, strip_sem, table_sem, own_sem,
    pair_send_sem, pair_recv_sem, line_send_sem, line_recv_sem, core_send_sem, core_recv_sem
):
    me = lax.axis_index("fs")
    pol = lax.axis_index("pol")
    half = lax.rem(pol, 2)
    partner = {"pol": pol + 1 - 2 * half}
    facet_local = strip_ref.shape[0]
    slots = everyone_ref.shape[2] // 2
    span = min(SPAN, facet_local)
    pairs = span // 2

    order = []
    for group in range(facet_local // span):
        for pair in range(pairs):
            low = group * span + pairs - 1 - pair
            order.append((low, low + 2 * pair + 1))
    loads = [
        pltpu.make_async_copy(strips_ref.at[f], strip_ref.at[f], strip_sem.at[f])
        for f in range(facet_local)
    ]
    own = pltpu.make_async_copy(coords_ref, everyone_ref.at[me], own_sem)
    own.start()
    tables = [
        pltpu.make_async_copy(from_ref, to_ref, table_sem.at[i])
        for i, (from_ref, to_ref) in enumerate(
            [
                (tables_hbm.at[pl.ds(S + 1, 4)], mix_ref),
                (tables_hbm.at[pl.ds(0, S)], first_ref),
                (tables_hbm.at[S], second_ref),
            ]
        )
    ]
    tables[0].start()
    for i, (low, high) in enumerate(order):
        loads[low].start()
        loads[high].start()
        if i == 0:
            tables[1].start()
            tables[2].start()

    across = {"fs": flip(me, 1)}
    line = {h: {"fs": flip(me, 2 * h)} for h in range(1, device_count // 2)}
    barrier = pltpu.get_barrier_semaphore()
    for peer in [partner, across] + list(line.values()):
        pl.semaphore_signal(barrier, inc=1, device_id=peer, device_id_type=pl.DeviceIdType.MESH)

    def send(source, peer, send_sem, recv_sem, index):
        piece = everyone_ref.at[source, :, pl.ds(half * slots, slots)]
        copy = pltpu.make_async_remote_copy(
            src_ref=piece,
            dst_ref=piece,
            send_sem=send_sem.at[index],
            recv_sem=recv_sem.at[index],
            device_id=peer,
            device_id_type=pl.DeviceIdType.MESH,
        )
        copy.start()
        return copy

    along = {}
    crossed = {}
    handed = []

    def to_partner(mask):
        handed.append(send(flip(me, mask), partner, core_send_sem, core_recv_sem, mask - 1))

    def relay(steps):
        for h in steps:
            along[h].wait_recv()
            crossed[h] = send(flip(me, 2 * h), across, pair_send_sem, pair_recv_sem, h)
            to_partner(2 * h)

    def hand_on():
        for h in line:
            crossed[h].wait_recv()
            to_partner(2 * h + 1)

    pl.semaphore_wait(barrier, device_count // 2 + 1)
    own.wait()
    crossed[0] = send(me, across, pair_send_sem, pair_recv_sem, 0)
    for h in line:
        along[h] = send(me, line[h], line_send_sem, line_recv_sem, h - 1)

    tables[0].wait()
    mix = jnp.concatenate(
        [jnp.concatenate([mix_ref[2 * i], mix_ref[2 * i + 1]], axis=1) for i in range(2)], axis=0
    )

    def lanes(pieces):
        return jnp.concatenate(pieces, axis=1).astype(jnp.bfloat16)

    for group in range(facet_local // span):
        for pair in range(pairs):
            low, high = order[group * pairs + pair]
            loads[low].wait()
            loads[high].wait()

            def join(i, carry, low=low, high=high, pair=pair):
                rows = pl.ds(pl.multiple_of(i * CHUNK, CHUNK), CHUNK)
                both = jnp.dot(
                    jnp.concatenate([strip_ref[low, rows, :], strip_ref[high, rows, :]], axis=1),
                    mix,
                    preferred_element_type=jnp.float32,
                )
                for t in range(CHUNK // W):
                    to = pl.ds((i * (CHUNK // W) + t) * PITCH, W)
                    for part in range(2):
                        mixed_ref[2 * pair + part, to, :] = both[
                            W * t : W * (t + 1), LANES * part : LANES * (part + 1)
                        ]
                return carry

            lax.fori_loop(0, FH // CHUNK, join, 0)
        if group == 0:
            tables[1].wait()
            tables[2].wait()

        def put(to_ref, rows, product):
            for pair in range(pairs):
                for part in range(2):
                    to_ref[2 * pair + part, rows, :] = product[
                        W * part : W * (part + 1), LANES * pair : LANES * (pair + 1)
                    ]

        def take(from_ref, rows):
            return jnp.concatenate(
                [lanes([from_ref[2 * q + part, rows, :] for q in range(pairs)]) for part in range(2)],
                axis=0,
            )

        def first(i, carry):
            for u in range(UNROLL):
                rows = pl.ds(i * UNROLL + u, W, stride=PITCH)
                put(
                    turned_ref,
                    rows,
                    jnp.dot(
                        first_ref[i * UNROLL + u],
                        take(mixed_ref, rows),
                        preferred_element_type=jnp.float32,
                    ),
                )
            return carry

        lax.fori_loop(0, S // UNROLL, first, 0)
        if group == 0:
            relay(list(line)[:1])
            crossed[0].wait_recv()
            to_partner(1)

        def second(i, carry):
            for u in range(UNROLL):
                k = i * UNROLL + u
                put(
                    mixed_ref,
                    pl.ds(k, S, stride=PITCH),
                    jnp.dot(
                        second_ref[...],
                        take(turned_ref, pl.ds(k * PITCH, S)),
                        preferred_element_type=jnp.float32,
                    ),
                )
            return carry

        lax.fori_loop(0, W // UNROLL, second, 0)
        if group == 0:
            relay(list(line)[1:])
        if group == facet_local // span - 1:
            hand_on()

        def third(i, carry, group=group):
            for u in range(2):
                s = i * 2 + u
                out_ref[s, pl.ds(group * 2 * W, 2 * W), :] = take(mixed_ref, pl.ds(s * PITCH, W))
            return carry

        lax.fori_loop(0, S // 2, third, 0)

    for copy in handed:
        copy.wait_recv()
    for copy in list(along.values()) + list(crossed.values()) + handed:
        copy.wait_send()
    gathered_ref[...] = everyone_ref[...]


def transform(strips, coords, device_count):
    vmem = pl.BlockSpec(memory_space=pltpu.VMEM)
    hbm = pl.BlockSpec(memory_space=pltpu.HBM)
    facet_local = strips.shape[0]
    span = min(SPAN, facet_local)
    scratch = pltpu.VMEM((span, S * PITCH, LANES), jnp.float32)
    kept = S * facet_local * 2 * W * W * 2 + device_count * coords.size * 4 + SLACK
    return pl.pallas_call(
        functools.partial(transform_kernel, device_count),
        out_shape=[
            jax.ShapeDtypeStruct((S, facet_local // span * 2 * W, span * W), jnp.bfloat16),
            jax.ShapeDtypeStruct((device_count,) + coords.shape, jnp.float32),
        ],
        in_specs=[hbm] * 3,
        out_specs=[vmem, vmem],
        scratch_shapes=[
            pltpu.VMEM((facet_local, FH, LANES), jnp.bfloat16),
            pltpu.VMEM((S, 2 * W, 2 * W), jnp.bfloat16),
            pltpu.VMEM((4, 2 * W, 2 * W), jnp.bfloat16),
            pltpu.VMEM((2 * S, 2 * S), jnp.bfloat16),
            scratch,
            scratch,
            pltpu.VMEM((device_count,) + coords.shape, jnp.float32),
            pltpu.SemaphoreType.DMA((facet_local,)),
            pltpu.SemaphoreType.DMA((3,)),
            pltpu.SemaphoreType.DMA,
            pltpu.SemaphoreType.DMA((device_count // 2,)),
            pltpu.SemaphoreType.DMA((device_count // 2,)),
            pltpu.SemaphoreType.DMA((device_count // 2 - 1,)),
            pltpu.SemaphoreType.DMA((device_count // 2 - 1,)),
            pltpu.SemaphoreType.DMA((device_count - 1,)),
            pltpu.SemaphoreType.DMA((device_count - 1,)),
        ],
        compiler_params=pltpu.CompilerParams(
            vmem_limit_bytes=VMEM_BYTES - kept, collective_id=0, has_side_effects=True
        ),
        cost_estimate=pl.CostEstimate(
            flops=5 * 10**9, bytes_accessed=16 * 2**20, transcendentals=0
        ),
    )(
        strips,
        pltpu.with_memory_space_constraint(jnp.asarray(transform_tables(), jnp.bfloat16), pltpu.HBM),
        pltpu.with_memory_space_constraint(coords, pltpu.HBM),
    )


def predict_kernel(
    facet_local, device_count, index_ref, owners_ref, counts_ref, coords_ref, windows_ref,
    limit_ref, kept_ref, sent_ref, out_ref, table_0_ref, table_1_ref, row_0_ref,
    row_1_ref, place_ref, load_ref, loads_ref
):
    lane = out_ref.shape[3]
    subgrids = owners_ref.shape[0]
    half, capacity = kept_ref.shape[:2]
    span = min(SPAN, facet_local)
    groups = facet_local // span
    steps = span // 2
    first = index_ref[0] * facet_local
    unit = 1.0 / SG
    row_middle = (lax.div(first, R) * W).astype(jnp.float32) + (0.5 * (W - 1) - SG // 2)
    col_middle = (lax.rem(first, R) * W).astype(jnp.float32) + (0.5 * (span * W - 1) - SG // 2)
    ramp = lax.broadcasted_iota(jnp.int32, (8, lane), 0).astype(jnp.float32)
    fine = (ramp + 0.5) * unit
    second = ramp >= 4.0
    kind = jnp.where(second, ramp - 4.0, ramp)
    col_pick = jnp.where(kind == 1.0, 0.0, col_middle + (kind - 2.0) * (span * W))
    col_pick = jnp.where(kind == 0.0, 8.0, col_pick) * unit
    row_pick = jnp.where(kind == 0.0, 0.0, jnp.where(kind == 1.0, 8.0, row_middle)) * unit
    out_ref[...] = jnp.zeros_like(out_ref)

    def clear(ref):
        def body(i, carry):
            ref[i] = 0
            return carry

        lax.fori_loop(0, ref.shape[0], body, 0)

    clear(loads_ref)
    clear(limit_ref)
    me = index_ref[0]

    def rank(s, total):
        owner = owners_ref[s]
        load = loads_ref[owner]
        loads_ref[owner] = load + 1
        count = counts_ref[s]
        offset = owner ^ me
        load_ref[s] = load
        place_ref[s] = ((offset & 1) * half + (offset >> 1)) * capacity + load

        @pl.when(owner == me)
        def _():
            limit_ref[load] = count

        return total + lax.div(count + 1, 2)

    total = lax.fori_loop(0, subgrids, rank, 0, unroll=8)

    def following(s, b):
        items = []
        for _ in range(PAIRS):
            items.append((s, b))
            done = b + 2 >= counts_ref[s]
            end = jnp.logical_and(done, s == subgrids - 1)
            b = jnp.where(end, b, jnp.where(done, 0, b + 2))
            s = jnp.where(done, jnp.minimum(s + 1, subgrids - 1), s)
        return items, (s, b)

    def tables(u, refs, s, b):
        table_ref, row_ref = refs
        owner, load = owners_ref[s], load_ref[s]
        at = [[coords_ref[owner, axis, load, pl.ds(b + h, 1), :] for h in range(2)] for axis in range(2)]
        x, y = [jnp.where(second, one[1], one[0]) for one in at]
        picked = phase(x * row_pick + y * col_pick)
        row_ref[u, 2, :16] = jnp.concatenate(picked, axis=0)
        for h in range(2):
            col_step, row_step = [
                [jnp.broadcast_to(part[4 * h + i : 4 * h + i + 1], (8, lane)) for part in picked]
                for i in range(2)
            ]
            cols = chain(phase(at[1][h] * fine), col_step, steps * W // 8)
            entries = []
            for k in range(steps):
                some = cols[W // 8 * k : W // 8 * (k + 1)]
                entries += [cos for cos, _ in some] + [sin for _, sin in some]
            table_ref[u, h] = jnp.concatenate(entries, axis=0).astype(jnp.bfloat16)
            rows = chain(phase(at[0][h] * fine), row_step, W // 16)
            row_ref[u, h] = jnp.concatenate([cos for cos, _ in rows] + [sin for _, sin in rows], axis=0)

    def predict(u, refs, s, b):
        table_ref, row_ref = refs
        table = jnp.concatenate([table_ref[u, 0], table_ref[u, 1]], axis=1)
        grid = jnp.dot(windows_ref[s], table, preferred_element_type=jnp.float32)
        place = place_ref[s]
        for h in range(2):
            real = imag = None
            for g in range(groups):
                sums = []
                for part in range(2):
                    total = None
                    for k in range(W // 8):
                        at = (2 * g + part) * W + 8 * k
                        term = grid[at : at + 8, h * lane : (h + 1) * lane] * row_ref[
                            u, h, 8 * k : 8 * k + 8, :
                        ]
                        total = term if total is None else total + term
                    sums.append(total)
                at = 4 * h + 2 + g
                cos, sin = row_ref[u, 2, at : at + 1, :], row_ref[u, 2, 8 + at : 9 + at, :]
                more_real = sums[0] * cos + sums[1] * sin
                more_imag = sums[1] * cos - sums[0] * sin
                real = more_real if real is None else real + more_real
                imag = more_imag if imag is None else imag + more_imag
            out_ref[place, 0, pl.ds(b + h, 1), :] = jnp.sum(real, axis=0, keepdims=True)
            out_ref[place, 1, pl.ds(b + h, 1), :] = jnp.sum(imag, axis=0, keepdims=True)

    turns = [(table_0_ref, row_0_ref), (table_1_ref, row_1_ref)]
    items, after = following(0, 0)
    for u, (s, b) in enumerate(items):
        tables(u, turns[0], s, b)

    def step(i, carry):
        items, after = carry
        for turn in range(2):
            for u, (s, b) in enumerate(items):
                predict(u, turns[turn], s, b)
            items, after = following(*after)
            for u, (s, b) in enumerate(items):
                tables(u, turns[1 - turn], s, b)
        return items, after

    lax.fori_loop(0, lax.div(total + 2 * PAIRS - 1, 2 * PAIRS), step, (items, after))
    kept_ref[...] = out_ref[: half * capacity].reshape(kept_ref.shape)
    sent_ref[...] = out_ref[half * capacity :].reshape(sent_ref.shape).astype(jnp.bfloat16)


def predict(windows, owners, counts, coords, device_index, facet_local):
    device_count, _, capacity, max_blocks, lane = coords.shape
    smem = pl.BlockSpec(memory_space=pltpu.SMEM)
    vmem = pl.BlockSpec(memory_space=pltpu.VMEM)
    slots = (capacity, 2, max_blocks, lane)
    return pl.pallas_call(
        functools.partial(predict_kernel, facet_local, device_count),
        out_shape=[
            jax.ShapeDtypeStruct((capacity,), jnp.int32),
            jax.ShapeDtypeStruct((device_count // 2,) + slots, jnp.float32),
            jax.ShapeDtypeStruct((device_count // 2,) + slots, jnp.bfloat16),
        ],
        in_specs=[smem, smem, smem, vmem, vmem],
        out_specs=[smem, vmem, vmem],
        scratch_shapes=[
            pltpu.VMEM((device_count * capacity,) + slots[1:], jnp.float32),
            pltpu.VMEM((PAIRS, 2, windows.shape[2], lane), jnp.bfloat16),
            pltpu.VMEM((PAIRS, 2, windows.shape[2], lane), jnp.bfloat16),
            pltpu.VMEM((PAIRS, 3, W, lane), jnp.float32),
            pltpu.VMEM((PAIRS, 3, W, lane), jnp.float32),
            pltpu.SMEM((owners.shape[0],), jnp.int32),
            pltpu.SMEM((owners.shape[0],), jnp.int32),
            pltpu.SMEM((device_count,), jnp.int32),
        ],
        compiler_params=pltpu.CompilerParams(
            vmem_limit_bytes=16 * 2**20
        ),
        cost_estimate=pl.CostEstimate(
            flops=2 * 10**10, bytes_accessed=2**20, transcendentals=0
        ),
    )(device_index.reshape(1), owners, counts, coords, windows)


def finish_kernel(
    parts, pols, limit_ref, stations_hbm, table_ref, kept_ref, cross_ref, out_ref, pair_ref, line_ref,
    partial_ref, station_ref, rows_ref, jones_ref, total_ref, sent_ref, station_sem, pair_send_sem,
    pair_recv_sem, line_send_sem, line_recv_sem, pol_send_sem, pol_recv_sem
):
    me = lax.axis_index("fs")
    pol = lax.axis_index("pol")
    half = kept_ref.shape[0]
    capacity, _, max_blocks, lane = total_ref.shape
    share = capacity // parts
    shares = [pl.ds(part * share, share) for part in range(parts)]
    across = {"fs": flip(me, 1)}
    line = [{"fs": flip(me, 2 * h)} for h in range(1, half)]
    pol_peers = [{"pol": lax.rem(pol + step, pols)} for step in range(1, pols)]
    stations = pltpu.make_async_copy(stations_hbm, station_ref, station_sem)
    stations.start()
    barrier = pltpu.get_barrier_semaphore()
    for peer in [across] + line + pol_peers:
        pl.semaphore_signal(
            barrier, inc=1, device_id=peer, device_id_type=pl.DeviceIdType.MESH
        )
    pl.semaphore_wait(barrier, half + pols - 1)

    def send(from_ref, to_ref, send_sem, recv_sem, peer):
        copy = pltpu.make_async_remote_copy(
            src_ref=from_ref,
            dst_ref=to_ref,
            send_sem=send_sem,
            recv_sem=recv_sem,
            device_id=peer,
            device_id_type=pl.DeviceIdType.MESH,
        )
        copy.start()
        return copy

    order = [(part, h) for part in range(parts) for h in reversed(range(half))]
    crossing = {
        (part, h): send(
            cross_ref.at[h, shares[part]],
            pair_ref.at[h, shares[part]],
            pair_send_sem.at[part, h],
            pair_recv_sem.at[part, h],
            across,
        )
        for part, h in order
    }
    stations.wait()
    chunks = table_ref.shape[1] // lane
    firsts = [4 * lax.div(pol, 2), 4 * lax.rem(pol, 2)]
    for row in range(table_ref.shape[0]):
        for chunk in range(chunks):
            at = row * chunks + chunk
            rows_ref[at : at + 1, :] = table_ref[row : row + 1, chunk * lane : (chunk + 1) * lane]

    def look_up(load, carry):
        for side in range(2):
            ids = station_ref[load, pl.ds(side, max_blocks, stride=2), :]
            low = ids & (lane - 1)
            high = ids >> (lane.bit_length() - 1)
            for row in range(4):
                entry = None
                for chunk in range(chunks):
                    source = jnp.broadcast_to(
                        rows_ref[pl.ds((firsts[side] + row) * chunks + chunk, 1), :],
                        (max_blocks, lane),
                    )
                    got = jnp.take_along_axis(source, low, axis=1, mode="promise_in_bounds")
                    entry = got if entry is None else jnp.where(high == chunk, got, entry)
                jones_ref[load, 4 * side + row] = entry
        return carry

    lax.fori_loop(0, capacity, look_up, 0)
    along = {}
    for part, h in order:
        slots = shares[part]
        crossing[part, h].wait_recv()
        joined = kept_ref[h, slots] + pair_ref[h, slots].astype(jnp.float32)
        if h == 0:
            total_ref[slots] = joined
            continue
        partial_ref[h - 1, slots] = joined.astype(jnp.bfloat16)
        along[part, h] = send(
            partial_ref.at[h - 1, slots],
            line_ref.at[h - 1, slots],
            line_send_sem.at[part, h - 1],
            line_recv_sem.at[part, h - 1],
            line[h - 1],
        )
    exchanged = {}
    for part, slots in enumerate(shares):
        total = total_ref[slots]
        for h in range(1, half):
            along[part, h].wait_recv()
            total = total + line_ref[h - 1, slots].astype(jnp.float32)
        total_ref[slots] = total
        sent_ref[pol, slots] = total.astype(jnp.bfloat16)
        for i, peer in enumerate(pol_peers):
            mine = sent_ref.at[pol, slots]
            exchanged[part, i] = send(
                mine, mine, pol_send_sem.at[part, i], pol_recv_sem.at[part, i], peer
            )
    block = lax.broadcasted_iota(jnp.int32, (max_blocks, lane), 0)

    def product(a, b):
        return (a[0] * b[0] - a[1] * b[1], a[0] * b[1] + a[1] * b[0])

    def correct(load, carry):
        jones = [jones_ref[load, i] for i in range(8)]
        real = jnp.zeros((max_blocks, lane), jnp.float32)
        imag = jnp.zeros((max_blocks, lane), jnp.float32)
        for row in range(2):
            for col in range(2):
                comp = 2 * row + col
                visible = [
                    jnp.where(
                        pol == comp, total_ref[load, i], sent_ref[comp, load, i].astype(jnp.float32)
                    )
                    for i in range(2)
                ]
                step = product((jones[2 * row], jones[2 * row + 1]), visible)
                step = product(step, (jones[4 + 2 * col], -jones[5 + 2 * col]))
                real = real + step[0]
                imag = imag + step[1]
        keep = block < limit_ref[load]
        out_ref[0, load] = jnp.where(keep, real, 0.0)
        out_ref[1, load] = jnp.where(keep, imag, 0.0)
        return carry

    for part in range(parts):
        for i in range(len(pol_peers)):
            exchanged[part, i].wait_recv()
        lax.fori_loop(part * share, (part + 1) * share, correct, 0)
    for copies in (crossing, along, exchanged):
        for copy in copies.values():
            copy.wait_send()


def finish(limit, kept, sent, station_ids, table, pols):
    half = kept.shape[0]
    slots = kept.shape[1:]
    capacity, _, max_blocks, lane = slots
    parts = max(1, min(SHARES, 16 // half))
    smem = pl.BlockSpec(memory_space=pltpu.SMEM)
    vmem = pl.BlockSpec(memory_space=pltpu.VMEM)
    hbm = pl.BlockSpec(memory_space=pltpu.HBM)
    return pl.pallas_call(
        functools.partial(finish_kernel, parts, pols),
        out_shape=jax.ShapeDtypeStruct((2, capacity, max_blocks, lane), jnp.float32),
        in_specs=[smem, hbm, vmem, vmem, vmem],
        out_specs=vmem,
        scratch_shapes=[
            pltpu.VMEM((half,) + slots, jnp.bfloat16),
            pltpu.VMEM((half - 1,) + slots, jnp.bfloat16),
            pltpu.VMEM((half - 1,) + slots, jnp.bfloat16),
            pltpu.VMEM((capacity, 2 * max_blocks, lane), jnp.int32),
            pltpu.VMEM((table.size // lane, lane), jnp.float32),
            pltpu.VMEM((capacity, 8, max_blocks, lane), jnp.float32),
            pltpu.VMEM(slots, jnp.float32),
            pltpu.VMEM((pols,) + slots, jnp.bfloat16),
            pltpu.SemaphoreType.DMA,
            pltpu.SemaphoreType.DMA((parts, half)),
            pltpu.SemaphoreType.DMA((parts, half)),
            pltpu.SemaphoreType.DMA((parts, half - 1)),
            pltpu.SemaphoreType.DMA((parts, half - 1)),
            pltpu.SemaphoreType.DMA((parts, pols - 1)),
            pltpu.SemaphoreType.DMA((parts, pols - 1)),
        ],
        compiler_params=pltpu.CompilerParams(
            vmem_limit_bytes=8 * 2**20, collective_id=1, has_side_effects=True
        ),
    )(
        limit,
        pltpu.with_memory_space_constraint(
            station_ids.reshape(capacity, 2 * max_blocks, lane), pltpu.HBM
        ),
        table,
        kept,
        sent,
    )


def on_device(facets, owners, counts, coords, station_ids, jones_table):
    device_index = lax.axis_index("fs").astype(jnp.int32)
    device_count, pols = lax.axis_size("fs"), lax.axis_size("pol")
    windows, all_coords = transform(facets[0], coords, device_count)
    limit, kept, sent = predict(
        windows, owners, counts, all_coords, device_index, facets.shape[1]
    )
    return finish(limit, kept, sent, station_ids, jones_table, pols)[None]


def solution(mesh):
    return jax.shard_map(
        on_device,
        mesh=mesh,
        in_specs=(
            P("pol", "fs", None, None),
            P(),
            P(),
            P(None, "fs", None, None),
            P("fs", None, None, None),
            P(),
        ),
        out_specs=P("pol", None, "fs", None, None),
        check_vma=False,
    )
```

```python
import functools
import math

import jax
import jax.numpy as jnp
import numpy as np
from jax import lax
from jax.experimental import pallas as pl
from jax.experimental.pallas import tpu as pltpu
from jax.sharding import PartitionSpec as P

R = 8
W = 64
S = 64
FH = 4096
SG = 512
LANES = 128
SPAN = 4
PITCH = 65
CHUNK = 2048
UNROLL = 64
PAIRS = 3
SHARES = 2
VMEM_BYTES = 67043328
SLACK = 13000 * 1024


def fit(values, terms):
    series = np.polynomial.chebyshev.Chebyshev.interpolate(
        lambda square: values(np.sqrt(np.maximum(square, 1e-12))), terms - 1, domain=[0.0, 0.25]
    )
    return [float(c) for c in series.convert(kind=np.polynomial.Polynomial).coef]


SIN_COEFS = fit(lambda r: np.sin(np.pi * r) / r, 5)
COS_COEFS = fit(lambda r: np.cos(np.pi * r), 5)


def unit_circle(turns):
    return np.exp(-2j * np.pi * turns)


def as_real(table):
    return np.concatenate(
        [
            np.concatenate([table.real, -table.imag], axis=-1),
            np.concatenate([table.imag, table.real], axis=-1),
        ],
        axis=-2,
    )


def mix_table():
    table = np.zeros((4 * W, 4 * W))
    col = np.arange(W)
    mirror = W - 1 - col
    a_real, a_imag, b_real, b_imag = mirror, W + mirror, 2 * W + col, 3 * W + col
    table[b_real, col] = table[a_real, col] = 1.0
    table[b_imag, W + col] = 1.0
    table[a_imag, W + col] = -1.0
    table[b_imag, 2 * W + col] = table[a_imag, 2 * W + col] = 1.0
    table[b_real, 3 * W + col] = -1.0
    table[a_real, 3 * W + col] = 1.0
    return table


def first_tables():
    n1 = np.arange(S)[:, None, None]
    k1 = np.arange(W)[None, :, None]
    n2 = np.arange(W)[None, None, :]
    rows = unit_circle((k1 * n2 % W) / W + (n1 * k1 % FH) / FH)
    upper, lower = rows[:, W // 2 :], rows[:, W // 2 - 1 :: -1]
    return as_real(np.concatenate([upper + lower, -1j * (upper - lower)], axis=1))


def second_table():
    index = np.arange(S)
    table = unit_circle((index[:, None] * index[None, :] % S) / S)
    return as_real(table) / (math.sqrt(FH) * SG)


def transform_tables():
    mix = mix_table().reshape(2, 2 * W, 2, 2 * W).transpose(0, 2, 1, 3).reshape(4, 2 * W, 2 * W)
    return np.concatenate([first_tables(), second_table()[None], mix])


def horner(coefs, square):
    total = jnp.full_like(square, coefs[-1])
    for coef in coefs[-2::-1]:
        total = total * square + coef
    return total


def phase(turns):
    rest = turns - jnp.round(turns)
    square = rest * rest
    half_cos = horner(COS_COEFS, square)
    half_sin = horner(SIN_COEFS, square) * rest
    double = half_sin + half_sin
    return 1.0 - double * half_sin, double * half_cos


def twice(left, right):
    return (left[0] * right[0] - left[1] * right[1], left[1] * right[0] + left[0] * right[1])


def chain(start, step, count):
    terms = [start, twice(start, step)]
    double = step[0] + step[0]
    while len(terms) < count:
        (last_cos, last_sin), (cos, sin) = terms[-2:]
        terms.append((double * cos - last_cos, double * sin - last_sin))
    return terms


def flip(index, mask):
    bit = 1
    flipped = index
    while bit <= mask:
        if mask & bit:
            flipped = flipped + bit * (1 - 2 * lax.rem(lax.div(index, bit), 2))
        bit *= 2
    return flipped


def transform_kernel(
    device_count, strips_ref, tables_hbm, coords_ref, out_ref, gathered_ref,
    strip_ref, first_ref, mix_ref, second_ref, mixed_ref, turned_ref, everyone_ref, strip_sem, table_sem, own_sem,
    pair_send_sem, pair_recv_sem, line_send_sem, line_recv_sem, core_send_sem, core_recv_sem
):
    me = lax.axis_index("fs")
    pol = lax.axis_index("pol")
    half = lax.rem(pol, 2)
    partner = {"pol": pol + 1 - 2 * half}
    facet_local = strip_ref.shape[0]
    slots = everyone_ref.shape[2] // 2
    span = min(SPAN, facet_local)
    pairs = span // 2

    order = []
    for group in range(facet_local // span):
        for pair in range(pairs):
            low = group * span + pairs - 1 - pair
            order.append((low, low + 2 * pair + 1))
    loads = [
        pltpu.make_async_copy(strips_ref.at[f], strip_ref.at[f], strip_sem.at[f])
        for f in range(facet_local)
    ]
    own = pltpu.make_async_copy(coords_ref, everyone_ref.at[me], own_sem)
    own.start()
    tables = [
        pltpu.make_async_copy(from_ref, to_ref, table_sem.at[i])
        for i, (from_ref, to_ref) in enumerate(
            [
                (tables_hbm.at[pl.ds(S + 1, 4)], mix_ref),
                (tables_hbm.at[pl.ds(0, S)], first_ref),
                (tables_hbm.at[S], second_ref),
            ]
        )
    ]
    tables[0].start()
    for i, (low, high) in enumerate(order):
        loads[low].start()
        loads[high].start()
        if i == 0:
            tables[1].start()
            tables[2].start()

    across = {"fs": flip(me, 1)}
    line = {h: {"fs": flip(me, 2 * h)} for h in range(1, device_count // 2)}
    barrier = pltpu.get_barrier_semaphore()
    for peer in [partner, across] + list(line.values()):
        pl.semaphore_signal(barrier, inc=1, device_id=peer, device_id_type=pl.DeviceIdType.MESH)

    def send(source, peer, send_sem, recv_sem, index):
        piece = everyone_ref.at[source, :, pl.ds(half * slots, slots)]
        copy = pltpu.make_async_remote_copy(
            src_ref=piece,
            dst_ref=piece,
            send_sem=send_sem.at[index],
            recv_sem=recv_sem.at[index],
            device_id=peer,
            device_id_type=pl.DeviceIdType.MESH,
        )
        copy.start()
        return copy

    along = {}
    crossed = {}
    handed = []

    def to_partner(mask):
        handed.append(send(flip(me, mask), partner, core_send_sem, core_recv_sem, mask - 1))

    def relay(steps):
        for h in steps:
            along[h].wait_recv()
            crossed[h] = send(flip(me, 2 * h), across, pair_send_sem, pair_recv_sem, h)
            to_partner(2 * h)

    def hand_on():
        for h in line:
            crossed[h].wait_recv()
            to_partner(2 * h + 1)

    pl.semaphore_wait(barrier, device_count // 2 + 1)
    own.wait()
    crossed[0] = send(me, across, pair_send_sem, pair_recv_sem, 0)
    for h in line:
        along[h] = send(me, line[h], line_send_sem, line_recv_sem, h - 1)

    tables[0].wait()
    mix = jnp.concatenate(
        [jnp.concatenate([mix_ref[2 * i], mix_ref[2 * i + 1]], axis=1) for i in range(2)], axis=0
    )

    def lanes(pieces):
        return jnp.concatenate(pieces, axis=1).astype(jnp.bfloat16)

    for group in range(facet_local // span):
        for pair in range(pairs):
            low, high = order[group * pairs + pair]
            loads[low].wait()
            loads[high].wait()

            def join(i, carry, low=low, high=high, pair=pair):
                rows = pl.ds(pl.multiple_of(i * CHUNK, CHUNK), CHUNK)
                both = jnp.dot(
                    jnp.concatenate([strip_ref[low, rows, :], strip_ref[high, rows, :]], axis=1),
                    mix,
                    preferred_element_type=jnp.float32,
                )
                for t in range(CHUNK // W):
                    to = pl.ds((i * (CHUNK // W) + t) * PITCH, W)
                    for part in range(2):
                        mixed_ref[2 * pair + part, to, :] = both[
                            W * t : W * (t + 1), LANES * part : LANES * (part + 1)
                        ]
                return carry

            lax.fori_loop(0, FH // CHUNK, join, 0)
        if group == 0:
            tables[1].wait()
            tables[2].wait()

        def put(to_ref, rows, product):
            for pair in range(pairs):
                for part in range(2):
                    to_ref[2 * pair + part, rows, :] = product[
                        W * part : W * (part + 1), LANES * pair : LANES * (pair + 1)
                    ]

        def take(from_ref, rows):
            return jnp.concatenate(
                [lanes([from_ref[2 * q + part, rows, :] for q in range(pairs)]) for part in range(2)],
                axis=0,
            )

        def first(i, carry):
            for u in range(UNROLL):
                rows = pl.ds(i * UNROLL + u, W, stride=PITCH)
                put(
                    turned_ref,
                    rows,
                    jnp.dot(
                        first_ref[i * UNROLL + u],
                        take(mixed_ref, rows),
                        preferred_element_type=jnp.float32,
                    ),
                )
            return carry

        lax.fori_loop(0, S // UNROLL, first, 0)
        if group == 0:
            relay(list(line)[:1])
            crossed[0].wait_recv()
            to_partner(1)

        def second(i, carry):
            for u in range(UNROLL):
                k = i * UNROLL + u
                put(
                    mixed_ref,
                    pl.ds(k, S, stride=PITCH),
                    jnp.dot(
                        second_ref[...],
                        take(turned_ref, pl.ds(k * PITCH, S)),
                        preferred_element_type=jnp.float32,
                    ),
                )
            return carry

        lax.fori_loop(0, W // UNROLL, second, 0)
        if group == 0:
            relay(list(line)[1:])
        if group == facet_local // span - 1:
            hand_on()

        def third(i, carry, group=group):
            for u in range(8):
                s = i * 8 + u
                out_ref[s, pl.ds(group * 2 * W, 2 * W), :] = take(mixed_ref, pl.ds(s * PITCH, W))
            return carry

        lax.fori_loop(0, S // 8, third, 0)

    for copy in handed:
        copy.wait_recv()
    for copy in list(along.values()) + list(crossed.values()) + handed:
        copy.wait_send()
    gathered_ref[...] = everyone_ref[...]


def transform(strips, coords, device_count):
    vmem = pl.BlockSpec(memory_space=pltpu.VMEM)
    hbm = pl.BlockSpec(memory_space=pltpu.HBM)
    facet_local = strips.shape[0]
    span = min(SPAN, facet_local)
    scratch = pltpu.VMEM((span, (S + 1) * PITCH, LANES), jnp.float32)
    kept = S * facet_local * 2 * W * W * 2 + device_count * coords.size * 4 + SLACK
    return pl.pallas_call(
        functools.partial(transform_kernel, device_count),
        out_shape=[
            jax.ShapeDtypeStruct((S, facet_local // span * 2 * W, span * W), jnp.bfloat16),
            jax.ShapeDtypeStruct((device_count,) + coords.shape, jnp.float32),
        ],
        in_specs=[hbm] * 3,
        out_specs=[vmem, vmem],
        scratch_shapes=[
            pltpu.VMEM((facet_local, FH, LANES), jnp.bfloat16),
            pltpu.VMEM((S, 2 * W, 2 * W), jnp.bfloat16),
            pltpu.VMEM((4, 2 * W, 2 * W), jnp.bfloat16),
            pltpu.VMEM((2 * S, 2 * S), jnp.bfloat16),
            scratch,
            scratch,
            pltpu.VMEM((device_count,) + coords.shape, jnp.float32),
            pltpu.SemaphoreType.DMA((facet_local,)),
            pltpu.SemaphoreType.DMA((3,)),
            pltpu.SemaphoreType.DMA,
            pltpu.SemaphoreType.DMA((device_count // 2,)),
            pltpu.SemaphoreType.DMA((device_count // 2,)),
            pltpu.SemaphoreType.DMA((device_count // 2 - 1,)),
            pltpu.SemaphoreType.DMA((device_count // 2 - 1,)),
            pltpu.SemaphoreType.DMA((device_count - 1,)),
            pltpu.SemaphoreType.DMA((device_count - 1,)),
        ],
        compiler_params=pltpu.CompilerParams(
            vmem_limit_bytes=VMEM_BYTES - kept, collective_id=0, has_side_effects=True
        ),
        cost_estimate=pl.CostEstimate(
            flops=5 * 10**9, bytes_accessed=16 * 2**20, transcendentals=0
        ),
    )(
        strips,
        pltpu.with_memory_space_constraint(jnp.asarray(transform_tables(), jnp.bfloat16), pltpu.HBM),
        pltpu.with_memory_space_constraint(coords, pltpu.HBM),
    )


def predict_kernel(
    facet_local, device_count, index_ref, owners_ref, counts_ref, coords_ref, windows_ref,
    limit_ref, kept_ref, sent_ref, out_ref, table_0_ref, table_1_ref, row_0_ref,
    row_1_ref, place_ref, load_ref, loads_ref
):
    lane = out_ref.shape[3]
    subgrids = owners_ref.shape[0]
    half, capacity = kept_ref.shape[:2]
    span = min(SPAN, facet_local)
    groups = facet_local // span
    steps = span // 2
    first = index_ref[0] * facet_local
    unit = 1.0 / SG
    row_middle = (lax.div(first, R) * W).astype(jnp.float32) + (0.5 * (W - 1) - SG // 2)
    col_middle = (lax.rem(first, R) * W).astype(jnp.float32) + (0.5 * (span * W - 1) - SG // 2)
    ramp = lax.broadcasted_iota(jnp.int32, (8, lane), 0).astype(jnp.float32)
    fine = (ramp + 0.5) * unit
    second = ramp >= 4.0
    kind = jnp.where(second, ramp - 4.0, ramp)
    col_pick = jnp.where(kind == 1.0, 0.0, col_middle + (kind - 2.0) * (span * W))
    col_pick = jnp.where(kind == 0.0, 8.0, col_pick) * unit
    row_pick = jnp.where(kind == 0.0, 0.0, jnp.where(kind == 1.0, 8.0, row_middle)) * unit
    out_ref[...] = jnp.zeros_like(out_ref)

    def clear(ref):
        def body(i, carry):
            ref[i] = 0
            return carry

        lax.fori_loop(0, ref.shape[0], body, 0)

    clear(loads_ref)
    clear(limit_ref)
    me = index_ref[0]

    def rank(s, total):
        owner = owners_ref[s]
        load = loads_ref[owner]
        loads_ref[owner] = load + 1
        count = counts_ref[s]
        offset = owner ^ me
        load_ref[s] = load
        place_ref[s] = ((offset & 1) * half + (offset >> 1)) * capacity + load

        @pl.when(owner == me)
        def _():
            limit_ref[load] = count

        return total + lax.div(count + 1, 2)

    total = lax.fori_loop(0, subgrids, rank, 0, unroll=8)

    def following(s, b):
        items = []
        for _ in range(PAIRS):
            items.append((s, b))
            done = b + 2 >= counts_ref[s]
            end = jnp.logical_and(done, s == subgrids - 1)
            b = jnp.where(end, b, jnp.where(done, 0, b + 2))
            s = jnp.where(done, jnp.minimum(s + 1, subgrids - 1), s)
        return items, (s, b)

    def tables(u, refs, s, b):
        table_ref, row_ref = refs
        owner, load = owners_ref[s], load_ref[s]
        at = [[coords_ref[owner, axis, load, pl.ds(b + h, 1), :] for h in range(2)] for axis in range(2)]
        x, y = [jnp.where(second, one[1], one[0]) for one in at]
        picked = phase(x * row_pick + y * col_pick)
        row_ref[u, 2, :16] = jnp.concatenate(picked, axis=0)
        for h in range(2):
            col_step, row_step = [
                [jnp.broadcast_to(part[4 * h + i : 4 * h + i + 1], (8, lane)) for part in picked]
                for i in range(2)
            ]
            cols = chain(phase(at[1][h] * fine), col_step, steps * W // 8)
            entries = []
            for k in range(steps):
                some = cols[W // 8 * k : W // 8 * (k + 1)]
                entries += [cos for cos, _ in some] + [sin for _, sin in some]
            table_ref[u, h] = jnp.concatenate(entries, axis=0).astype(jnp.bfloat16)
            rows = chain(phase(at[0][h] * fine), row_step, W // 16)
            row_ref[u, h] = jnp.concatenate([cos for cos, _ in rows] + [sin for _, sin in rows], axis=0)

    def predict(u, refs, s, b):
        table_ref, row_ref = refs
        table = jnp.concatenate([table_ref[u, 0], table_ref[u, 1]], axis=1)
        grid = jnp.dot(windows_ref[s], table, preferred_element_type=jnp.float32)
        place = place_ref[s]
        for h in range(2):
            real = imag = None
            for g in range(groups):
                sums = []
                for part in range(2):
                    total = None
                    for k in range(W // 8):
                        at = (2 * g + part) * W + 8 * k
                        term = grid[at : at + 8, h * lane : (h + 1) * lane] * row_ref[
                            u, h, 8 * k : 8 * k + 8, :
                        ]
                        total = term if total is None else total + term
                    sums.append(total)
                at = 4 * h + 2 + g
                cos, sin = row_ref[u, 2, at : at + 1, :], row_ref[u, 2, 8 + at : 9 + at, :]
                more_real = sums[0] * cos + sums[1] * sin
                more_imag = sums[1] * cos - sums[0] * sin
                real = more_real if real is None else real + more_real
                imag = more_imag if imag is None else imag + more_imag
            out_ref[place, 0, pl.ds(b + h, 1), :] = jnp.sum(real, axis=0, keepdims=True)
            out_ref[place, 1, pl.ds(b + h, 1), :] = jnp.sum(imag, axis=0, keepdims=True)

    turns = [(table_0_ref, row_0_ref), (table_1_ref, row_1_ref)]
    items, after = following(0, 0)
    for u, (s, b) in enumerate(items):
        tables(u, turns[0], s, b)

    def step(i, carry):
        items, after = carry
        for turn in range(2):
            for u, (s, b) in enumerate(items):
                predict(u, turns[turn], s, b)
            items, after = following(*after)
            for u, (s, b) in enumerate(items):
                tables(u, turns[1 - turn], s, b)
        return items, after

    lax.fori_loop(0, lax.div(total + 2 * PAIRS - 1, 2 * PAIRS), step, (items, after))
    kept_ref[...] = out_ref[: half * capacity].reshape(kept_ref.shape)
    sent_ref[...] = out_ref[half * capacity :].reshape(sent_ref.shape).astype(jnp.bfloat16)


def predict(windows, owners, counts, coords, device_index, facet_local):
    device_count, _, capacity, max_blocks, lane = coords.shape
    smem = pl.BlockSpec(memory_space=pltpu.SMEM)
    vmem = pl.BlockSpec(memory_space=pltpu.VMEM)
    slots = (capacity, 2, max_blocks, lane)
    return pl.pallas_call(
        functools.partial(predict_kernel, facet_local, device_count),
        out_shape=[
            jax.ShapeDtypeStruct((capacity,), jnp.int32),
            jax.ShapeDtypeStruct((device_count // 2,) + slots, jnp.float32),
            jax.ShapeDtypeStruct((device_count // 2,) + slots, jnp.bfloat16),
        ],
        in_specs=[smem, smem, smem, vmem, vmem],
        out_specs=[smem, vmem, vmem],
        scratch_shapes=[
            pltpu.VMEM((device_count * capacity,) + slots[1:], jnp.float32),
            pltpu.VMEM((PAIRS, 2, windows.shape[2], lane), jnp.bfloat16),
            pltpu.VMEM((PAIRS, 2, windows.shape[2], lane), jnp.bfloat16),
            pltpu.VMEM((PAIRS, 3, W, lane), jnp.float32),
            pltpu.VMEM((PAIRS, 3, W, lane), jnp.float32),
            pltpu.SMEM((owners.shape[0],), jnp.int32),
            pltpu.SMEM((owners.shape[0],), jnp.int32),
            pltpu.SMEM((device_count,), jnp.int32),
        ],
        compiler_params=pltpu.CompilerParams(
            vmem_limit_bytes=16 * 2**20
        ),
        cost_estimate=pl.CostEstimate(
            flops=2 * 10**10, bytes_accessed=2**20, transcendentals=0
        ),
    )(device_index.reshape(1), owners, counts, coords, windows)


def finish_kernel(
    parts, pols, limit_ref, stations_hbm, table_ref, kept_ref, cross_ref, out_ref, pair_ref, line_ref,
    partial_ref, station_ref, rows_ref, jones_ref, total_ref, sent_ref, station_sem, pair_send_sem,
    pair_recv_sem, line_send_sem, line_recv_sem, pol_send_sem, pol_recv_sem
):
    me = lax.axis_index("fs")
    pol = lax.axis_index("pol")
    half = kept_ref.shape[0]
    capacity, _, max_blocks, lane = total_ref.shape
    share = capacity // parts
    shares = [pl.ds(part * share, share) for part in range(parts)]
    across = {"fs": flip(me, 1)}
    line = [{"fs": flip(me, 2 * h)} for h in range(1, half)]
    pol_peers = [{"pol": lax.rem(pol + step, pols)} for step in range(1, pols)]
    stations = pltpu.make_async_copy(stations_hbm, station_ref, station_sem)
    stations.start()
    barrier = pltpu.get_barrier_semaphore()
    for peer in [across] + line + pol_peers:
        pl.semaphore_signal(
            barrier, inc=1, device_id=peer, device_id_type=pl.DeviceIdType.MESH
        )
    pl.semaphore_wait(barrier, half + pols - 1)

    def send(from_ref, to_ref, send_sem, recv_sem, peer):
        copy = pltpu.make_async_remote_copy(
            src_ref=from_ref,
            dst_ref=to_ref,
            send_sem=send_sem,
            recv_sem=recv_sem,
            device_id=peer,
            device_id_type=pl.DeviceIdType.MESH,
        )
        copy.start()
        return copy

    order = [(part, h) for part in range(parts) for h in reversed(range(half))]
    crossing = {
        (part, h): send(
            cross_ref.at[h, shares[part]],
            pair_ref.at[h, shares[part]],
            pair_send_sem.at[part, h],
            pair_recv_sem.at[part, h],
            across,
        )
        for part, h in order
    }
    stations.wait()
    chunks = table_ref.shape[1] // lane
    firsts = [4 * lax.div(pol, 2), 4 * lax.rem(pol, 2)]
    for row in range(table_ref.shape[0]):
        for chunk in range(chunks):
            at = row * chunks + chunk
            rows_ref[at : at + 1, :] = table_ref[row : row + 1, chunk * lane : (chunk + 1) * lane]

    def look_up(load, carry):
        for side in range(2):
            ids = station_ref[load, pl.ds(side, max_blocks, stride=2), :]
            low = ids & (lane - 1)
            high = ids >> (lane.bit_length() - 1)
            for row in range(4):
                entry = None
                for chunk in range(chunks):
                    source = jnp.broadcast_to(
                        rows_ref[pl.ds((firsts[side] + row) * chunks + chunk, 1), :],
                        (max_blocks, lane),
                    )
                    got = jnp.take_along_axis(source, low, axis=1, mode="promise_in_bounds")
                    entry = got if entry is None else jnp.where(high == chunk, got, entry)
                jones_ref[load, 4 * side + row] = entry
        return carry

    lax.fori_loop(0, capacity, look_up, 0, unroll=2)
    along = {}
    for part, h in order:
        slots = shares[part]
        crossing[part, h].wait_recv()
        joined = kept_ref[h, slots] + pair_ref[h, slots].astype(jnp.float32)
        if h == 0:
            total_ref[slots] = joined
            continue
        partial_ref[h - 1, slots] = joined.astype(jnp.bfloat16)
        along[part, h] = send(
            partial_ref.at[h - 1, slots],
            line_ref.at[h - 1, slots],
            line_send_sem.at[part, h - 1],
            line_recv_sem.at[part, h - 1],
            line[h - 1],
        )
    exchanged = {}
    for part, slots in enumerate(shares):
        total = total_ref[slots]
        for h in range(1, half):
            along[part, h].wait_recv()
            total = total + line_ref[h - 1, slots].astype(jnp.float32)
        total_ref[slots] = total
        sent_ref[pol, slots] = total.astype(jnp.bfloat16)
        for i, peer in enumerate(pol_peers):
            mine = sent_ref.at[pol, slots]
            exchanged[part, i] = send(
                mine, mine, pol_send_sem.at[part, i], pol_recv_sem.at[part, i], peer
            )
    block = lax.broadcasted_iota(jnp.int32, (max_blocks, lane), 0)

    def product(a, b):
        return (a[0] * b[0] - a[1] * b[1], a[0] * b[1] + a[1] * b[0])

    def correct(load, carry):
        jones = [jones_ref[load, i] for i in range(8)]
        real = jnp.zeros((max_blocks, lane), jnp.float32)
        imag = jnp.zeros((max_blocks, lane), jnp.float32)
        for row in range(2):
            for col in range(2):
                comp = 2 * row + col
                visible = [
                    jnp.where(
                        pol == comp, total_ref[load, i], sent_ref[comp, load, i].astype(jnp.float32)
                    )
                    for i in range(2)
                ]
                step = product((jones[2 * row], jones[2 * row + 1]), visible)
                step = product(step, (jones[4 + 2 * col], -jones[5 + 2 * col]))
                real = real + step[0]
                imag = imag + step[1]
        keep = block < limit_ref[load]
        out_ref[0, load] = jnp.where(keep, real, 0.0)
        out_ref[1, load] = jnp.where(keep, imag, 0.0)
        return carry

    for part in range(parts):
        for i in range(len(pol_peers)):
            exchanged[part, i].wait_recv()
        lax.fori_loop(part * share, (part + 1) * share, correct, 0, unroll=2)
    for copies in (crossing, along, exchanged):
        for copy in copies.values():
            copy.wait_send()


def finish(limit, kept, sent, station_ids, table, pols):
    half = kept.shape[0]
    slots = kept.shape[1:]
    capacity, _, max_blocks, lane = slots
    parts = max(1, min(SHARES, 16 // half))
    smem = pl.BlockSpec(memory_space=pltpu.SMEM)
    vmem = pl.BlockSpec(memory_space=pltpu.VMEM)
    hbm = pl.BlockSpec(memory_space=pltpu.HBM)
    return pl.pallas_call(
        functools.partial(finish_kernel, parts, pols),
        out_shape=jax.ShapeDtypeStruct((2, capacity, max_blocks, lane), jnp.float32),
        in_specs=[smem, hbm, vmem, vmem, vmem],
        out_specs=vmem,
        scratch_shapes=[
            pltpu.VMEM((half,) + slots, jnp.bfloat16),
            pltpu.VMEM((half - 1,) + slots, jnp.bfloat16),
            pltpu.VMEM((half - 1,) + slots, jnp.bfloat16),
            pltpu.VMEM((capacity, 2 * max_blocks, lane), jnp.int32),
            pltpu.VMEM((table.size // lane, lane), jnp.float32),
            pltpu.VMEM((capacity, 8, max_blocks, lane), jnp.float32),
            pltpu.VMEM(slots, jnp.float32),
            pltpu.VMEM((pols,) + slots, jnp.bfloat16),
            pltpu.SemaphoreType.DMA,
            pltpu.SemaphoreType.DMA((parts, half)),
            pltpu.SemaphoreType.DMA((parts, half)),
            pltpu.SemaphoreType.DMA((parts, half - 1)),
            pltpu.SemaphoreType.DMA((parts, half - 1)),
            pltpu.SemaphoreType.DMA((parts, pols - 1)),
            pltpu.SemaphoreType.DMA((parts, pols - 1)),
        ],
        compiler_params=pltpu.CompilerParams(
            vmem_limit_bytes=8 * 2**20, collective_id=1, has_side_effects=True
        ),
    )(
        limit,
        pltpu.with_memory_space_constraint(
            station_ids.reshape(capacity, 2 * max_blocks, lane), pltpu.HBM
        ),
        table,
        kept,
        sent,
    )


def on_device(facets, owners, counts, coords, station_ids, jones_table):
    device_index = lax.axis_index("fs").astype(jnp.int32)
    device_count, pols = lax.axis_size("fs"), lax.axis_size("pol")
    windows, all_coords = transform(facets[0], coords, device_count)
    limit, kept, sent = predict(
        windows, owners, counts, all_coords, device_index, facets.shape[1]
    )
    return finish(limit, kept, sent, station_ids, jones_table, pols)[None]


def solution(mesh):
    return jax.shard_map(
        on_device,
        mesh=mesh,
        in_specs=(
            P("pol", "fs", None, None),
            P(),
            P(),
            P(None, "fs", None, None),
            P("fs", None, None, None),
            P(),
        ),
        out_specs=P("pol", None, "fs", None, None),
        check_vma=False,
    )
```
